32 devices in a mesh: grp: 2 (over y), gx: 4 (over z), gy: 4 (over x, core).
Axes of the slice: x: 2, y: 2, z: 4, core: 2. Of those that a mesh axis runs over, the one named last changes fastest.
Arguments:
- source: bfloat16 [512, 256, 128], P(('grp', 'gx'), 'gy'), parts along dimension 0, may hold values from -6 to 6
- field: bfloat16 [512, 256, 128], P(('grp', 'gx'), 'gy'), parts along dimension 0, may hold values from -3 to 3
- kerr: float32 [512, 256], P(('grp', 'gx'), 'gy'), parts along dimension 0, may hold values from 0.05 to 0.3
- wave: float32 [512, 256], P(('grp', 'gx'), 'gy'), parts along dimension 0, may hold values from 0.5 to 2
- leaf_ops: bfloat16 [16, 16, 256, 256], P('gx', 'gy'), may hold values from -0.375 to 0.375
- transfer_ops: float32 [4, 256, 64], P('gx', 'gy'), may hold values from 0 to 1
Outputs:
- updated: bfloat16 [512, 256, 128], P(('grp', 'gx'), 'gy'), parts along dimension 0
- residual: bfloat16 [512, 256, 128], P(('grp', 'gx'), 'gy'), parts along dimension 0
The draws below stay inside these ranges and needn't reach their ends.
There are 2 independent parts, one for each index of `grp`. The reference program is written for one: setup_inputs(seed, part) draws one part's arguments, and reference() takes and returns one part's arrays. A program takes and returns all parts, laid end to end along the dimension named above; an argument that names none is the same for every part. Nothing has to cross between parts.
All inputs are finite; a program needn't handle non-finite values.
Results may differ from the reference program's by a relative error of at most 0.015.
Values may be sent and summed in bfloat16 or wider, within the bound.
No kernel may reach another device: no remote copies, remote signals or barrier semaphores. Data moves between devices by JAX's collectives and lax.ppermute only.
A program may use at most 64 MiB of HBM per device.

```python
import math
import jax
import jax.numpy as jnp
from jax import lax

Q = 16
P_SIZE = 256
LX = 4
LY = 4
B = 128
XD = 64
YD = 64
NXP = 256
NYP = 256
N_GX = 4
N_GY = 4


def draw_transfer_ops(key, part):
    random_key_list = jax.random.split(key, 6)
    row_count = N_GY * YD
    growth_rates = jnp.exp(jax.random.uniform(random_key_list[0], (row_count,), jnp.float32, math.log(0.5 / N_GX), math.log(2.0)))
    spread_width = jax.random.uniform(random_key_list[1], (N_GX, 1, 1), jnp.float32, 0.5, 1.5)
    pulse_trains = jnp.where(jax.random.uniform(random_key_list[2], (N_GX, 1, 1), jnp.float32) < 3.0 / N_GX, 0.6, 1.0)
    damping_factor = jnp.exp(-growth_rates[None, :, None] * spread_width) * pulse_trains
    row_pos = (jnp.arange(row_count) % YD)[:, None].astype(jnp.float32)
    col_pos = jnp.arange(YD)[None, :].astype(jnp.float32)
    distance = jnp.abs(row_pos - col_pos)
    on_diagonal = distance < 0.5
    rough_factor = jax.random.uniform(random_key_list[3], (N_GX, row_count, YD), jnp.float32, 0.5, 1.0)
    kernel_width = jax.random.uniform(random_key_list[4], (N_GX, row_count, 1), jnp.float32, 2.0, 8.0)
    off_entries = jnp.where(on_diagonal[None], 0.0, rough_factor * jnp.exp(-distance[None] / kernel_width))
    off_total = jnp.sum(off_entries, axis=2, keepdims=True)
    keep_share = jax.random.uniform(random_key_list[5], (N_GX, row_count, 1), jnp.float32, 0.6, 0.75)
    mixed_map = jnp.where(on_diagonal[None], keep_share, (1.0 - keep_share) * off_entries / off_total)
    return damping_factor * mixed_map


def block_scale(rng, extent, cuts, low, largest):
    factor_of, own = 1.0, jax.random.fold_in(rng, 6)
    for dim, shards_of in cuts:
        draws = jnp.exp(jax.random.uniform(jax.random.fold_in(own, dim), (shards_of,), jnp.float32, low / len(cuts), largest / len(cuts)))
        factor_of = factor_of * jnp.repeat(draws, extent[dim] // shards_of).reshape([-1 if axis == dim else 1 for axis in range(len(extent))])
    return factor_of


def scatter_about(own_key, extent, spread, reach, pieces=(), kind=jnp.bfloat16):
    gain = block_scale(own_key, extent, pieces, -0.22, 0.18) if pieces else 1.0
    values = jax.random.normal(own_key, extent, jnp.float32) * spread * gain
    return jnp.minimum(jnp.maximum(values, -reach), reach).astype(kind)


def setup_inputs(seed: int = 0, part: int = 0) -> dict:
    key_of = jax.random.split(jax.random.key(seed), 7)
    part_splits = jax.random.split(jax.random.fold_in(key_of[6], part), 7)
    source = scatter_about(part_splits[0], (NXP, NYP, B), 1.0, 6.0, ((0, 4), (1, 4)))
    field = scatter_about(part_splits[1], (NXP, NYP, B), 0.7, 3.0, ((0, 4), (1, 4)))
    kerr = jnp.clip(jnp.exp(math.log(0.3) - 1.7917595 * jax.random.uniform(part_splits[2], (NXP, NYP), jnp.float32) ** block_scale(part_splits[2], (NXP, NYP), ((0, 4), (1, 4)), -0.2, 0.2)), 0.05, 0.3)
    wave = jnp.clip(0.5 + 1.5 * jax.random.uniform(part_splits[3], (NXP, NYP), jnp.float32) ** block_scale(part_splits[3], (NXP, NYP), ((0, 4), (1, 4)), -0.2, 0.2), 0.5, 2.0)
    leaf_ops = scatter_about(key_of[4], (N_GX * LX, N_GY * LY, P_SIZE, P_SIZE), P_SIZE ** -0.5, 0.375, ((0, 4), (1, 4)))
    transfer_ops = draw_transfer_ops(jax.random.fold_in(key_of[6], 71), part)
    return dict(source=source, field=field, kerr=kerr, wave=wave, leaf_ops=leaf_ops, transfer_ops=transfer_ops)


lift_weight = 0.3


def reference(source, field, kerr, wave, leaf_ops, transfer_ops):
    source_f = source.astype(jnp.float32)
    field_f = field.astype(jnp.float32)
    kerr_source = (source_f - kerr[:, :, None] * field_f * field_f * field_f).astype(jnp.bfloat16)
    leaves = kerr_source.reshape(N_GX * LX, Q, N_GY * LY, Q, B).transpose(0, 2, 1, 3, 4).reshape(N_GX * LX, N_GY * LY, P_SIZE, B)

    def solve_row(pair):
        return jnp.einsum("bpq,bqn->bpn", pair[0].astype(jnp.float32), pair[1].astype(jnp.float32), precision=lax.Precision.HIGHEST)

    solved = lax.map(solve_row, (leaf_ops, leaves))
    particular_solution = solved.reshape(N_GX * LX, N_GY * LY, Q, Q, B).transpose(0, 2, 1, 3, 4).reshape(NXP, NYP, B)
    slabs = particular_solution.reshape(N_GX, XD, N_GY, YD, B)
    right_face = slabs[:, -1]
    left_face = slabs[:, 0]
    operators = transfer_ops.reshape(N_GX, N_GY, YD, YD)

    def step_up(state, inputs):
        oper_d, face_d = inputs
        nxt = jnp.einsum("gij,gjb->gib", oper_d, state, precision=lax.Precision.HIGHEST) + face_d
        return nxt, state

    def step_down(state, inputs):
        oper_d, face_d = inputs
        nxt = jnp.einsum("gji,gjb->gib", oper_d, state, precision=lax.Precision.HIGHEST) + face_d
        return nxt, state

    start = jnp.zeros((N_GY, YD, B), jnp.float32)
    _, w_in = lax.scan(step_up, start, (operators, right_face))
    _, z_in = lax.scan(step_down, start, (operators, left_face), reverse=True)
    position = jnp.arange(XD).astype(jnp.float32)
    left_prof = ((XD - position) / XD)[None, :, None, None, None]
    right_prof = ((position + 1.0) / XD)[None, :, None, None, None]
    lifted = slabs + lift_weight * (left_prof * w_in[:, None] + right_prof * z_in[:, None])
    updated = lifted.reshape(NXP, NYP, B).astype(jnp.bfloat16)
    values = updated.astype(jnp.float32)
    padded_patches = jnp.pad(values, ((1, 1), (1, 1), (0, 0)))
    laplacian_operator = padded_patches[2:, 1:-1] + padded_patches[:-2, 1:-1] + padded_patches[1:-1, 2:] + padded_patches[1:-1, :-2] - 4.0 * values
    residual = laplacian_operator + wave[:, :, None] * values + kerr[:, :, None] * values * values * values - source_f
    return updated, residual.astype(jnp.bfloat16)
```

```python
import functools

import jax
import jax.numpy as jnp
from jax import lax
from jax.experimental import pallas as pl
from jax.experimental.pallas import tpu as pltpu
from jax.sharding import PartitionSpec as P

lift_weight = 0.3
f32, bf16 = jnp.float32, jnp.bfloat16
VMEM = pl.BlockSpec(memory_space=pltpu.VMEM)
ANY = pl.BlockSpec(memory_space=pl.ANY)


def call(body, outs, ins, out_specs=None, scratch=(), cost=(0, 0), aliases=None):
    def run(*args):
        return pl.pallas_call(
            body,
            out_shape=outs,
            in_specs=ins,
            out_specs=out_specs if out_specs is not None else jax.tree.map(lambda _: VMEM, outs),
            scratch_shapes=scratch,
            input_output_aliases=aliases or {},
            compiler_params=pltpu.CompilerParams(vmem_limit_bytes=24 << 20),
            cost_estimate=pl.CostEstimate(
                flops=cost[0], bytes_accessed=cost[1], transcendentals=0
            ),
        )(*args)

    return run


def matmul(a, b):
    return jnp.dot(a, b, preferred_element_type=f32)


def kerr_column(source, field, kerr):
    s, f = source.astype(f32), field.astype(f32)
    return (s - kerr * f * f * f).astype(bf16)


def faces_body(
    half, points, source, field, kerr, leaf_ops, transfer, msg, edge, src, fld, ops, sems
):
    lx, ly, pts, _ = leaf_ops.shape
    xs, ys, cols = source.shape
    copies = []
    for e, (x0, a, r0) in enumerate(((0, 0, 0), (xs - points, lx - 1, pts - points))):
        group = [
            pltpu.make_async_copy(source.at[pl.ds(x0, points)], src.at[e], sems.at[e, 0]),
            pltpu.make_async_copy(field.at[pl.ds(x0, points)], fld.at[e], sems.at[e, 1]),
            pltpu.make_async_copy(
                leaf_ops.at[a, :, pl.ds(r0, points), :], ops.at[e], sems.at[e, 2]
            ),
        ]
        for c in group:
            c.start()
        copies.append(group)
    is_a = lax.axis_index("gx") < half
    own = transfer[0]
    x_map = jnp.where(is_a, own, own.T).astype(bf16)
    faces = []
    for e in range(2):
        x0 = 0 if e == 0 else xs - points
        kt = kerr[x0 : x0 + points, :].T
        for c in copies[e]:
            c.wait()
        for q in range(points):
            edge[e, q] = kerr_column(src[e, q], fld[e, q], kt[:, q : q + 1])
        rows = []
        for b in range(ly):
            rhs = edge[e, :, b * points : (b + 1) * points, :].reshape(pts, cols)
            rows.append(matmul(ops[e, b], rhs))
        faces.append(jnp.concatenate(rows, axis=0).astype(bf16))
    left, right = faces
    msg[0:ys, :] = jnp.where(is_a, right, left)
    msg[ys : 2 * ys, :] = jnp.where(is_a, left, right)
    msg[2 * ys :, :] = jnp.concatenate([x_map[: ys // 2], x_map[ys // 2 :]], axis=1)


def split_message(m, ys):
    packed = m[2 * ys :]
    return m[:ys], m[ys : 2 * ys], jnp.concatenate([packed[:, :ys], packed[:, ys:]], axis=0)


def leaves_body(points, edge, source, field, kerr, leaf_ops, part, ends, rhs_all):
    lx, ly, pts, _ = leaf_ops.shape
    xs, ys, cols = source.shape
    kt = kerr[...].T
    for a in range(lx):
        for q in range(points):
            x = a * points + q
            if a == 0:
                col = edge[0, q]
            elif a == lx - 1:
                col = edge[1, q]
            else:
                col = kerr_column(source[x], field[x], kt[:, x : x + 1])
            rhs_all[x] = col
        for b in range(ly):
            rhs = rhs_all[a * points : (a + 1) * points, b * points : (b + 1) * points, :]
            out = matmul(leaf_ops[a, b], rhs.reshape(pts, cols))
            for q in range(points):
                r = (a * points + q) * ys + b * points
                part[r : r + points, :] = out[q * points : (q + 1) * points, :]
    ends[0:xs, :] = part[pl.ds(0, xs, stride=ys), :]
    ends[xs:, :] = part[pl.ds(ys - 1, xs, stride=ys), :]


def compose_body(count, xs, own, got, msg, keep, inner_map):
    ys = own.shape[1] // 2
    place = lax.axis_index("gx")
    inner = (place == count // 2 - 1) | (place == count // 2)
    f_own, g_own, x_own = split_message(own[...], ys)
    f_got, g_got, x_got = split_message(got[...], ys)
    f_in = jnp.where(inner, f_own, f_got)
    g_in = jnp.where(inner, g_own, g_got)
    x_in = jnp.where(inner, x_own, x_got)
    f_out = jnp.where(inner, f_got, f_own)
    reach = matmul(x_in, f_out) + f_in.astype(f32)
    msg[0:ys, :] = reach.astype(bf16)
    msg[ys:, :] = (f_in.astype(f32) + (lift_weight / xs) * f_out.astype(f32)).astype(bf16)
    keep[0] = f_out.astype(f32)
    keep[1] = g_in.astype(f32)
    keep[2] = reach
    inner_map[...] = x_in


def weights_body(kerr, wave, kerr_b, wave_b):
    xs, ys, cols = kerr_b.shape
    kt, wt = kerr[...].T, wave[...].T
    for x in range(xs):
        kerr_b[x] = jnp.broadcast_to(kt[:, x : x + 1], (ys, cols))
        wave_b[x] = jnp.broadcast_to(wt[:, x : x + 1], (ys, cols))


def profiles(xs):
    i = lax.broadcasted_iota(jnp.int32, (xs, 1), 0).astype(f32)
    return (xs - i) / xs, (i + 1.0) / xs


def edge_columns(ends, w, z, pair, cross):
    xs = pair.shape[0]
    ys = w.shape[0]
    lp, rp = profiles(xs)
    low = ends[0:xs, :] + (lp * w[0:1, :] + rp * z[0:1, :])
    high = ends[xs:, :] + (lp * w[ys - 1 : ys, :] + rp * z[ys - 1 : ys, :])
    even = lax.axis_index("gy") % 2 == 0
    pair[...] = jnp.where(even, high, low).astype(bf16)
    cross[...] = jnp.where(even, low, high).astype(bf16)


def finish_body(count, got, keep, inner_map, ends, waves, halo, pair, cross):
    ys = got.shape[0] // 2
    xs = pair.shape[0]
    place = lax.axis_index("gx")
    inner = (place == count // 2 - 1) | (place == count // 2)
    is_a = place < count // 2
    back = got[0:ys, :]
    e_got = got[ys:, :].astype(f32)
    f_out, g_in, reach = keep[0], keep[1], keep[2]
    t = lax.dot_general(
        inner_map[...], back, (((0,), (0,)), ((), ())), preferred_element_type=f32
    ) + g_in
    back = back.astype(f32)
    forward = jnp.where(inner, f_out, 0.0)
    backward = jnp.where(inner, back, t)
    w = lift_weight * jnp.where(is_a, forward, backward)
    z = lift_weight * jnp.where(is_a, backward, forward)
    waves[0] = w
    waves[1] = z
    toward = jnp.where(
        inner,
        e_got + lift_weight * reach,
        g_in + lift_weight * (f_out + back * (1.0 / xs)),
    )
    away = jnp.where(inner, f_out + lift_weight * t, 0.0)
    halo[0] = jnp.where(is_a, away, toward).astype(bf16)
    halo[1] = jnp.where(is_a, toward, away).astype(bf16)
    edge_columns(ends, w, z, pair, cross)


def ends_body(ends, waves, pair, cross):
    edge_columns(ends, waves[0], waves[1], pair, cross)


def stencil(rows, ys):
    i = lax.broadcasted_iota(jnp.int32, (rows, rows), 0)
    j = lax.broadcasted_iota(jnp.int32, (rows, rows), 1)
    near = (abs(i - j) == 1) & (i // ys == j // ys)
    return jnp.where(i == j, -4.0, jnp.where(near, 1.0, 0.0)).astype(bf16)


def update_body(
    strip, group, part, waves, halo, kerr_b, wave_b, source, updated, residual, strips,
    u, res, sems,
):
    xs, ys, cols = source.shape
    w, z = waves[0], waves[1]
    u[0] = halo[0]
    u[xs + 1] = halo[1]

    def lift(x, _):
        xf = x.astype(f32)
        row = pl.multiple_of(x * ys, ys)
        lp, rp = (xs - xf) * (1.0 / xs), (xf + 1.0) * (1.0 / xs)
        u[x + 1] = (part[pl.ds(row, ys), :] + (lp * w + rp * z)).astype(bf16)
        return 0

    lax.fori_loop(0, xs, lift, 0, unroll=4)
    out_u = pltpu.make_async_copy(u.at[pl.ds(1, xs)], updated, sems.at[0])
    out_u.start()
    taps = stencil(group * ys, ys)

    def one(i, _):
        x = i * group
        mid = u[pl.ds(x + 1, group)]
        near = matmul(taps, mid.reshape(group * ys, cols)).reshape(group, ys, cols)
        m = mid.astype(f32)
        above = u[pl.ds(x, group)].astype(f32)
        below = u[pl.ds(x + 2, group)].astype(f32)
        k, v = kerr_b[pl.ds(x, group)], wave_b[pl.ds(x, group)]
        s = source[pl.ds(x, group)].astype(f32)
        r = (near + (above + below)) + (m * (v + k * (m * m)) - s)
        strips[0, pl.ds(x, group)] = r[:, :strip, :]
        strips[1, pl.ds(x, group)] = r[:, ys - strip :, :]
        res[pl.ds(x, group)] = r[:, strip : ys - strip, :].astype(bf16)
        return 0

    lax.fori_loop(0, xs // group, one, 0)
    out_r = pltpu.make_async_copy(res, residual.at[:, pl.ds(strip, ys - 2 * strip), :], sems.at[1])
    out_r.start()
    out_u.wait()
    out_r.wait()


def seam_body(count, strip, strips, pair, cross, _, residual, work, out, sems):
    xs, ys, cols = residual.shape
    g = lax.axis_index("gy")
    even = g % 2 == 0
    zero = jnp.zeros((), f32)
    p, c = pair[...].astype(f32), cross[...].astype(f32)
    low = jnp.where(g == 0, zero, jnp.where(even, c, p))
    high = jnp.where(g == count - 1, zero, jnp.where(even, p, c))
    for e, (row, add) in enumerate(((0, low), (strip - 1, high))):
        work[e] = strips[e].reshape(xs * strip, cols)
        at = pl.ds(row, xs, stride=strip)
        work[e, at, :] = work[e, at, :] + add
        out[e] = work[e].reshape(xs, strip, cols).astype(bf16)
        y0 = 0 if e == 0 else ys - strip
        pltpu.make_async_copy(
            out.at[e], residual.at[:, pl.ds(y0, strip), :], sems.at[e]
        ).start()
    for e in range(2):
        y0 = 0 if e == 0 else ys - strip
        pltpu.make_async_copy(
            out.at[e], residual.at[:, pl.ds(y0, strip), :], sems.at[e]
        ).wait()


def gathered_sweeps(message, ys, xs, count):
    place = lax.axis_index("gx")
    every = lax.all_gather(message, "gx").astype(f32)
    right, left = every[:, :ys], every[:, ys : 2 * ys]
    packed = every[:, 2 * ys :]
    maps = jnp.concatenate([packed[:, :, :ys], packed[:, :, ys:]], axis=1)
    start = jnp.zeros_like(right[0])
    exact = functools.partial(jnp.dot, precision=lax.Precision.HIGHEST)

    def up(state, inp):
        return exact(inp[0], state) + inp[1], state

    def down(state, inp):
        return exact(inp[0].T, state) + inp[1], state

    _, w = lax.scan(up, start, (maps, right))
    _, z = lax.scan(down, start, (maps, left), reverse=True)
    before, after = jnp.maximum(place - 1, 0), jnp.minimum(place + 1, count - 1)
    low = right[before] + lift_weight * (w[before] / xs + z[before])
    high = left[after] + lift_weight * (w[after] + z[after] / xs)
    low = jnp.where(place == 0, 0.0, low)
    high = jnp.where(place == count - 1, 0.0, high)
    return lift_weight * jnp.stack([w[place], z[place]]), jnp.stack([low, high]).astype(bf16)


def per_device(source, field, kerr, wave, leaf_ops, transfer_ops):
    xs, ys, cols = source.shape
    lx, ly, pts, _ = leaf_ops.shape
    points = xs // lx
    n_gx, n_gy = lax.axis_size("gx"), lax.axis_size("gy")
    doubling = n_gx == 4
    shape = jax.ShapeDtypeStruct
    dots = 2 * lx * ly * pts * pts * cols

    message, edge = call(
        functools.partial(faces_body, n_gx // 2 if doubling else n_gx, points),
        (shape((2 * ys + ys // 2, cols), bf16), shape((2, points, ys, cols), bf16)),
        [ANY, ANY, VMEM, ANY, VMEM],
        scratch=[
            pltpu.VMEM((2, points, ys, cols), bf16),
            pltpu.VMEM((2, points, ys, cols), bf16),
            pltpu.VMEM((2, ly, points, pts), bf16),
            pltpu.SemaphoreType.DMA((2, 3)),
        ],
        cost=(dots // 8, 2 << 20),
    )(source, field, kerr, leaf_ops, transfer_ops)

    if doubling:
        other = lax.ppermute(message, "gx", [(i, i ^ 1) for i in range(n_gx)])

    part, ends = call(
        functools.partial(leaves_body, points),
        (shape((xs * ys, cols), f32), shape((2 * xs, cols), f32)),
        [VMEM] * 5,
        scratch=[pltpu.VMEM((xs, ys, cols), bf16)],
        cost=(dots, 6 << 20),
    )(edge, source, field, kerr, leaf_ops)

    kerr_b, wave_b = call(
        weights_body,
        (shape((xs, ys, cols), f32), shape((xs, ys, cols), f32)),
        [VMEM] * 2,
        cost=(xs * ys * cols, 4 << 20),
    )(kerr, wave)

    column = shape((xs, cols), bf16)
    if doubling:
        reach, keep, inner_map = call(
            functools.partial(compose_body, n_gx, xs),
            (shape((2 * ys, cols), bf16), shape((3, ys, cols), f32), shape((ys, ys), bf16)),
            [VMEM] * 2,
        )(message, other)
        far = lax.ppermute(reach, "gx", [(i, i ^ 2) for i in range(n_gx)])
        waves, halo, pair, cross = call(
            functools.partial(finish_body, n_gx),
            (shape((2, ys, cols), f32), shape((2, ys, cols), bf16), column, column),
            [VMEM] * 4,
        )(far, keep, inner_map, ends)
    else:
        waves, halo = gathered_sweeps(message, ys, xs, n_gx)
        pair, cross = call(ends_body, (column, column), [VMEM] * 2)(ends, waves)

    pair_to = [(i, i + 1 - 2 * (i % 2)) for i in range(n_gy)]
    cross_to = [(i, (i - 1 + 2 * (i % 2)) % n_gy) for i in range(n_gy)]
    pair = lax.ppermute(pair, "gy", pair_to)
    cross = lax.ppermute(cross, "gy", cross_to)

    strip, group = 16, 4
    big = shape((xs, ys, cols), bf16)
    updated, residual, strips = call(
        functools.partial(update_body, strip, group),
        (big, big, shape((2, xs, strip, cols), f32)),
        [VMEM] * 6,
        out_specs=(ANY, ANY, VMEM),
        scratch=[
            pltpu.VMEM((xs + 2, ys, cols), bf16),
            pltpu.VMEM((xs, ys - 2 * strip, cols), bf16),
            pltpu.SemaphoreType.DMA((2,)),
        ],
        cost=(20 * xs * ys * cols, 10 << 20),
    )(part, waves, halo, kerr_b, wave_b, source)

    residual = call(
        functools.partial(seam_body, n_gy, strip),
        big,
        [VMEM, VMEM, VMEM, ANY],
        out_specs=ANY,
        scratch=[
            pltpu.VMEM((2, xs * strip, cols), f32),
            pltpu.VMEM((2, xs, strip, cols), bf16),
            pltpu.SemaphoreType.DMA((2,)),
        ],
        aliases={3: 0},
    )(strips, pair, cross, residual)
    return updated, residual


def solution(mesh):
    return jax.shard_map(
        per_device,
        mesh=mesh,
        in_specs=(
            P(("grp", "gx"), "gy", None),
            P(("grp", "gx"), "gy", None),
            P(("grp", "gx"), "gy"),
            P(("grp", "gx"), "gy"),
            P("gx", "gy", None, None),
            P("gx", "gy", None),
        ),
        out_specs=(P(("grp", "gx"), "gy", None), P(("grp", "gx"), "gy", None)),
        check_vma=False,
    )
```

```python
import functools

import jax
import jax.numpy as jnp
from jax import lax
from jax.experimental import pallas as pl
from jax.experimental.pallas import tpu as pltpu
from jax.sharding import PartitionSpec as P

lift_weight = 0.3
f32, bf16 = jnp.float32, jnp.bfloat16
VMEM = pl.BlockSpec(memory_space=pltpu.VMEM)
ANY = pl.BlockSpec(memory_space=pl.ANY)
HBM = pl.BlockSpec(memory_space=pltpu.HBM)


def call(body, outs, ins, out_specs=None, scratch=(), cost=(0, 0), aliases=None):
    def run(*args):
        return pl.pallas_call(
            body,
            out_shape=outs,
            in_specs=ins,
            out_specs=out_specs if out_specs is not None else jax.tree.map(lambda _: VMEM, outs),
            scratch_shapes=scratch,
            input_output_aliases=aliases or {},
            compiler_params=pltpu.CompilerParams(vmem_limit_bytes=24 << 20),
            cost_estimate=pl.CostEstimate(
                flops=cost[0], bytes_accessed=cost[1], transcendentals=0
            ),
        )(*args)

    return run


def in_hbm(x):
    return pltpu.with_memory_space_constraint(x, pltpu.HBM)


def matmul(a, b):
    return jnp.dot(a, b, preferred_element_type=f32)


def kerr_column(source, field, kerr):
    s, f = source.astype(f32), field.astype(f32)
    return (s - kerr * f * f * f).astype(bf16)


def faces_body(
    half, points, source, field, kerr_all, leaf_ops, transfer, msg, edge, src, fld, ops, kerr, own,
    sems, more,
):
    lx, ly, pts, _ = leaf_ops.shape
    xs, ys, cols = source.shape
    small = [
        pltpu.make_async_copy(kerr_all, kerr, more.at[0]),
        pltpu.make_async_copy(transfer.at[0], own, more.at[1]),
    ]
    small[0].start()
    copies = []
    for e, (x0, a, r0) in enumerate(((0, 0, 0), (xs - points, lx - 1, pts - points))):
        group = [
            pltpu.make_async_copy(source.at[pl.ds(x0, points)], src.at[e], sems.at[e, 0]),
            pltpu.make_async_copy(field.at[pl.ds(x0, points)], fld.at[e], sems.at[e, 1]),
            pltpu.make_async_copy(
                leaf_ops.at[a, :, pl.ds(r0, points), :], ops.at[e], sems.at[e, 2]
            ),
        ]
        for c in group:
            c.start()
        copies.append(group)
    small[1].start()
    is_a = lax.axis_index("gx") < half
    small[0].wait()
    faces = []
    for e in range(2):
        x0 = 0 if e == 0 else xs - points
        kt = kerr[x0 : x0 + points, :].T
        for c in copies[e]:
            c.wait()
        for q in range(points):
            edge[e, q] = kerr_column(src[e, q], fld[e, q], kt[:, q : q + 1])
        rows = []
        for b in range(ly):
            rhs = edge[e, :, b * points : (b + 1) * points, :].reshape(pts, cols)
            rows.append(matmul(ops[e, b], rhs))
        faces.append(jnp.concatenate(rows, axis=0).astype(bf16))
    left, right = faces
    small[1].wait()
    x_map = jnp.where(is_a, own[...], own[...].T).astype(bf16)
    msg[0:ys, :] = jnp.where(is_a, right, left)
    msg[ys : 2 * ys, :] = jnp.where(is_a, left, right)
    msg[2 * ys :, :] = jnp.concatenate([x_map[: ys // 2], x_map[ys // 2 :]], axis=1)


def split_message(m, ys):
    packed = m[2 * ys :]
    return m[:ys], m[ys : 2 * ys], jnp.concatenate([packed[:, :ys], packed[:, ys:]], axis=0)


def leaves_body(points, edge, source, field, kerr, leaf_ops, part, ends, rhs_all):
    lx, ly, pts, _ = leaf_ops.shape
    xs, ys, cols = source.shape
    kt = kerr[...].T
    for a in range(lx):
        for q in range(points):
            x = a * points + q
            if a == 0:
                col = edge[0, q]
            elif a == lx - 1:
                col = edge[1, q]
            else:
                col = kerr_column(source[x], field[x], kt[:, x : x + 1])
            rhs_all[x] = col
        for b in range(ly):
            rhs = rhs_all[a * points : (a + 1) * points, b * points : (b + 1) * points, :]
            out = matmul(leaf_ops[a, b], rhs.reshape(pts, cols))
            for q in range(points):
                r = (a * points + q) * ys + b * points
                part[r : r + points, :] = out[q * points : (q + 1) * points, :]
    ends[0:xs, :] = part[pl.ds(0, xs, stride=ys), :]
    ends[xs:, :] = part[pl.ds(ys - 1, xs, stride=ys), :]


def compose_body(count, xs, own, got, msg, keep, inner_map):
    ys = own.shape[1] // 2
    place = lax.axis_index("gx")
    inner = (place == count // 2 - 1) | (place == count // 2)
    f_own, g_own, x_own = split_message(own[...], ys)
    f_got, g_got, x_got = split_message(got[...], ys)
    f_in = jnp.where(inner, f_own, f_got)
    g_in = jnp.where(inner, g_own, g_got)
    x_in = jnp.where(inner, x_own, x_got)
    f_out = jnp.where(inner, f_got, f_own)
    reach = matmul(x_in, f_out) + f_in.astype(f32)
    msg[0:ys, :] = reach.astype(bf16)
    msg[ys:, :] = (f_in.astype(f32) + (lift_weight / xs) * f_out.astype(f32)).astype(bf16)
    keep[0] = f_out.astype(f32)
    keep[1] = g_in.astype(f32)
    keep[2] = reach
    inner_map[...] = x_in


def weights_body(kerr, wave, kerr_b, wave_b):
    xs, ys, cols = kerr_b.shape
    kt, wt = kerr[...].T, wave[...].T
    for x in range(xs):
        kerr_b[x] = jnp.broadcast_to(kt[:, x : x + 1], (ys, cols))
        wave_b[x] = jnp.broadcast_to(wt[:, x : x + 1], (ys, cols))


def profiles(xs):
    i = lax.broadcasted_iota(jnp.int32, (xs, 1), 0).astype(f32)
    return (xs - i) / xs, (i + 1.0) / xs


def edge_columns(ends, w, z, pair, cross):
    xs = pair.shape[0]
    ys = w.shape[0]
    lp, rp = profiles(xs)
    low = ends[0:xs, :] + (lp * w[0:1, :] + rp * z[0:1, :])
    high = ends[xs:, :] + (lp * w[ys - 1 : ys, :] + rp * z[ys - 1 : ys, :])
    even = lax.axis_index("gy") % 2 == 0
    pair[...] = jnp.where(even, high, low).astype(bf16)
    cross[...] = jnp.where(even, low, high).astype(bf16)


def finish_body(count, got, keep, inner_map, ends, waves, halo, pair, cross):
    ys = got.shape[0] // 2
    xs = pair.shape[0]
    place = lax.axis_index("gx")
    inner = (place == count // 2 - 1) | (place == count // 2)
    is_a = place < count // 2
    back = got[0:ys, :]
    e_got = got[ys:, :].astype(f32)
    f_out, g_in, reach = keep[0], keep[1], keep[2]
    t = lax.dot_general(
        inner_map[...], back, (((0,), (0,)), ((), ())), preferred_element_type=f32
    ) + g_in
    back = back.astype(f32)
    forward = jnp.where(inner, f_out, 0.0)
    backward = jnp.where(inner, back, t)
    w = lift_weight * jnp.where(is_a, forward, backward)
    z = lift_weight * jnp.where(is_a, backward, forward)
    waves[0] = w
    waves[1] = z
    toward = jnp.where(
        inner,
        e_got + lift_weight * reach,
        g_in + lift_weight * (f_out + back * (1.0 / xs)),
    )
    away = jnp.where(inner, f_out + lift_weight * t, 0.0)
    halo[0] = jnp.where(is_a, away, toward).astype(bf16)
    halo[1] = jnp.where(is_a, toward, away).astype(bf16)
    edge_columns(ends, w, z, pair, cross)


def ends_body(ends, waves, pair, cross):
    edge_columns(ends, waves[0], waves[1], pair, cross)


def stencil(rows, ys):
    i = lax.broadcasted_iota(jnp.int32, (rows, rows), 0)
    j = lax.broadcasted_iota(jnp.int32, (rows, rows), 1)
    near = (abs(i - j) == 1) & (i // ys == j // ys)
    return jnp.where(i == j, -4.0, jnp.where(near, 1.0, 0.0)).astype(bf16)


def update_body(
    strip, group, part, waves, halo, kerr_b, wave_b, source, updated, residual, strips,
    u, res, sems,
):
    xs, ys, cols = source.shape
    w, z = waves[0], waves[1]
    u[0] = halo[0]
    u[xs + 1] = halo[1]

    def lift(x, _):
        xf = x.astype(f32)
        row = pl.multiple_of(x * ys, ys)
        lp, rp = (xs - xf) * (1.0 / xs), (xf + 1.0) * (1.0 / xs)
        u[x + 1] = (part[pl.ds(row, ys), :] + (lp * w + rp * z)).astype(bf16)
        return 0

    lax.fori_loop(0, xs, lift, 0, unroll=4)
    out_u = pltpu.make_async_copy(u.at[pl.ds(1, xs)], updated, sems.at[0])
    out_u.start()
    taps = stencil(group * ys, ys)

    def one(i, _):
        x = i * group
        mid = u[pl.ds(x + 1, group)]
        near = matmul(taps, mid.reshape(group * ys, cols)).reshape(group, ys, cols)
        m = mid.astype(f32)
        above = u[pl.ds(x, group)].astype(f32)
        below = u[pl.ds(x + 2, group)].astype(f32)
        k, v = kerr_b[pl.ds(x, group)], wave_b[pl.ds(x, group)]
        s = source[pl.ds(x, group)].astype(f32)
        r = (near + (above + below)) + (m * (v + k * (m * m)) - s)
        strips[0, pl.ds(x, group)] = r[:, :strip, :]
        strips[1, pl.ds(x, group)] = r[:, ys - strip :, :]
        res[pl.ds(x, group)] = r[:, strip : ys - strip, :].astype(bf16)
        return 0

    lax.fori_loop(0, xs // group, one, 0)
    out_r = pltpu.make_async_copy(res, residual.at[:, pl.ds(strip, ys - 2 * strip), :], sems.at[1])
    out_r.start()
    out_u.wait()
    out_r.wait()


def seam_body(count, strip, strips, pair, cross, _, residual, work, out, sems):
    xs, ys, cols = residual.shape
    g = lax.axis_index("gy")
    even = g % 2 == 0
    zero = jnp.zeros((), f32)
    p, c = pair[...].astype(f32), cross[...].astype(f32)
    low = jnp.where(g == 0, zero, jnp.where(even, c, p))
    high = jnp.where(g == count - 1, zero, jnp.where(even, p, c))
    for e, (row, add) in enumerate(((0, low), (strip - 1, high))):
        work[e] = strips[e].reshape(xs * strip, cols)
        at = pl.ds(row, xs, stride=strip)
        work[e, at, :] = work[e, at, :] + add
        out[e] = work[e].reshape(xs, strip, cols).astype(bf16)
        y0 = 0 if e == 0 else ys - strip
        pltpu.make_async_copy(
            out.at[e], residual.at[:, pl.ds(y0, strip), :], sems.at[e]
        ).start()
    for e in range(2):
        y0 = 0 if e == 0 else ys - strip
        pltpu.make_async_copy(
            out.at[e], residual.at[:, pl.ds(y0, strip), :], sems.at[e]
        ).wait()


def gathered_sweeps(message, ys, xs, count):
    place = lax.axis_index("gx")
    every = lax.all_gather(message, "gx").astype(f32)
    right, left = every[:, :ys], every[:, ys : 2 * ys]
    packed = every[:, 2 * ys :]
    maps = jnp.concatenate([packed[:, :, :ys], packed[:, :, ys:]], axis=1)
    start = jnp.zeros_like(right[0])
    exact = functools.partial(jnp.dot, precision=lax.Precision.HIGHEST)

    def up(state, inp):
        return exact(inp[0], state) + inp[1], state

    def down(state, inp):
        return exact(inp[0].T, state) + inp[1], state

    _, w = lax.scan(up, start, (maps, right))
    _, z = lax.scan(down, start, (maps, left), reverse=True)
    before, after = jnp.maximum(place - 1, 0), jnp.minimum(place + 1, count - 1)
    low = right[before] + lift_weight * (w[before] / xs + z[before])
    high = left[after] + lift_weight * (w[after] + z[after] / xs)
    low = jnp.where(place == 0, 0.0, low)
    high = jnp.where(place == count - 1, 0.0, high)
    return lift_weight * jnp.stack([w[place], z[place]]), jnp.stack([low, high]).astype(bf16)


def per_device(source, field, kerr, wave, leaf_ops, transfer_ops):
    xs, ys, cols = source.shape
    lx, ly, pts, _ = leaf_ops.shape
    points = xs // lx
    n_gx, n_gy = lax.axis_size("gx"), lax.axis_size("gy")
    doubling = n_gx == 4
    shape = jax.ShapeDtypeStruct
    dots = 2 * lx * ly * pts * pts * cols

    message, edge = call(
        functools.partial(faces_body, n_gx // 2 if doubling else n_gx, points),
        (shape((2 * ys + ys // 2, cols), bf16), shape((2, points, ys, cols), bf16)),
        [HBM] * 5,
        scratch=[
            pltpu.VMEM((2, points, ys, cols), bf16),
            pltpu.VMEM((2, points, ys, cols), bf16),
            pltpu.VMEM((2, ly, points, pts), bf16),
            pltpu.VMEM((xs, ys), f32),
            pltpu.VMEM((ys, ys), f32),
            pltpu.SemaphoreType.DMA((2, 3)),
            pltpu.SemaphoreType.DMA((2,)),
        ],
        cost=(dots // 8, 2 << 20),
    )(*map(in_hbm, (source, field, kerr, leaf_ops, transfer_ops)))
    message, edge, source, field, kerr, wave, leaf_ops = lax.optimization_barrier(
        (message, edge, source, field, kerr, wave, leaf_ops)
    )

    if doubling:
        other = lax.ppermute(message, "gx", [(i, i ^ 1) for i in range(n_gx)])

    part, ends = call(
        functools.partial(leaves_body, points),
        (shape((xs * ys, cols), f32), shape((2 * xs, cols), f32)),
        [VMEM] * 5,
        scratch=[pltpu.VMEM((xs, ys, cols), bf16)],
        cost=(dots, 6 << 20),
    )(edge, source, field, kerr, leaf_ops)

    kerr_b, wave_b = call(
        weights_body,
        (shape((xs, ys, cols), f32), shape((xs, ys, cols), f32)),
        [VMEM] * 2,
        cost=(xs * ys * cols, 4 << 20),
    )(kerr, wave)

    column = shape((xs, cols), bf16)
    if doubling:
        other, part, ends = lax.optimization_barrier((other, part, ends))
        reach, keep, inner_map = call(
            functools.partial(compose_body, n_gx, xs),
            (shape((2 * ys, cols), bf16), shape((3, ys, cols), f32), shape((ys, ys), bf16)),
            [VMEM] * 2,
        )(message, other)
        far = lax.ppermute(reach, "gx", [(i, i ^ 2) for i in range(n_gx)])
        far, kerr_b, wave_b = lax.optimization_barrier((far, kerr_b, wave_b))
        waves, halo, pair, cross = call(
            functools.partial(finish_body, n_gx),
            (shape((2, ys, cols), f32), shape((2, ys, cols), bf16), column, column),
            [VMEM] * 4,
        )(far, keep, inner_map, ends)
    else:
        waves, halo = gathered_sweeps(message, ys, xs, n_gx)
        pair, cross = call(ends_body, (column, column), [VMEM] * 2)(ends, waves)

    pair_to = [(i, i + 1 - 2 * (i % 2)) for i in range(n_gy)]
    cross_to = [(i, (i - 1 + 2 * (i % 2)) % n_gy) for i in range(n_gy)]
    pair = lax.ppermute(pair, "gy", pair_to)
    cross = lax.ppermute(cross, "gy", cross_to)

    strip, group = 16, 4
    big = shape((xs, ys, cols), bf16)
    updated, residual, strips = call(
        functools.partial(update_body, strip, group),
        (big, big, shape((2, xs, strip, cols), f32)),
        [VMEM] * 6,
        out_specs=(ANY, ANY, VMEM),
        scratch=[
            pltpu.VMEM((xs + 2, ys, cols), bf16),
            pltpu.VMEM((xs, ys - 2 * strip, cols), bf16),
            pltpu.SemaphoreType.DMA((2,)),
        ],
        cost=(20 * xs * ys * cols, 10 << 20),
    )(part, waves, halo, kerr_b, wave_b, source)

    residual = call(
        functools.partial(seam_body, n_gy, strip),
        big,
        [VMEM, VMEM, VMEM, ANY],
        out_specs=ANY,
        scratch=[
            pltpu.VMEM((2, xs * strip, cols), f32),
            pltpu.VMEM((2, xs, strip, cols), bf16),
            pltpu.SemaphoreType.DMA((2,)),
        ],
        aliases={3: 0},
    )(strips, pair, cross, residual)
    return updated, residual


def solution(mesh):
    return jax.shard_map(
        per_device,
        mesh=mesh,
        in_specs=(
            P(("grp", "gx"), "gy", None),
            P(("grp", "gx"), "gy", None),
            P(("grp", "gx"), "gy"),
            P(("grp", "gx"), "gy"),
            P("gx", "gy", None, None),
            P("gx", "gy", None),
        ),
        out_specs=(P(("grp", "gx"), "gy", None), P(("grp", "gx"), "gy", None)),
        check_vma=False,
    )
```

```python
import functools

import jax
import jax.numpy as jnp
from jax import lax
from jax.experimental import pallas as pl
from jax.experimental.pallas import tpu as pltpu
from jax.sharding import PartitionSpec as P

lift_weight = 0.3
f32, bf16 = jnp.float32, jnp.bfloat16
VMEM = pl.BlockSpec(memory_space=pltpu.VMEM)
ANY = pl.BlockSpec(memory_space=pl.ANY)
HBM = pl.BlockSpec(memory_space=pltpu.HBM)


def call(body, outs, ins, out_specs=None, scratch=(), cost=(0, 0), aliases=None):
    def run(*args):
        return pl.pallas_call(
            body,
            out_shape=outs,
            in_specs=ins,
            out_specs=out_specs if out_specs is not None else jax.tree.map(lambda _: VMEM, outs),
            scratch_shapes=scratch,
            input_output_aliases=aliases or {},
            compiler_params=pltpu.CompilerParams(vmem_limit_bytes=24 << 20),
            cost_estimate=pl.CostEstimate(
                flops=cost[0], bytes_accessed=cost[1], transcendentals=0
            ),
        )(*args)

    return run


def in_hbm(x):
    return pltpu.with_memory_space_constraint(x, pltpu.HBM)


def matmul(a, b):
    return jnp.dot(a, b, preferred_element_type=f32)


def kerr_column(source, field, kerr):
    s, f = source.astype(f32), field.astype(f32)
    return (s - kerr * f * f * f).astype(bf16)


def faces_body(
    half, points, parts, source, field, kerr_all, leaf_ops, transfer, msg, edge, src, fld, ops,
    kerr, own, kb, sems, more,
):
    lx, ly, pts, _ = leaf_ops.shape
    xs, ys, cols = source.shape
    copy = pltpu.make_async_copy
    firsts = (0, xs - points)
    size = points // parts
    coef = copy(kerr_all, kerr, more.at[0])
    coef.start()
    pieces = {}
    for e, x0 in enumerate(firsts):
        for i in range(parts):
            at, here = pl.ds(x0 + i * size, size), pl.ds(i * size, size)
            pieces[e, i] = (
                copy(source.at[at], src.at[e, here], sems.at[e, 2 * i]),
                copy(field.at[at], fld.at[e, here], sems.at[e, 2 * i + 1]),
            )
            for c in pieces[e, i]:
                c.start(priority=e)
    rows_of = []
    for e, (a, r0) in enumerate(((0, 0), (lx - 1, pts - points))):
        rows_of.append(copy(leaf_ops.at[a, :, pl.ds(r0, points), :], ops.at[e], more.at[2 + e]))
        rows_of[e].start()
    matrix = copy(transfer.at[0], own, more.at[1])
    matrix.start()
    is_a = lax.axis_index("gx") < half
    coef.wait()
    kts = [kerr[x0 : x0 + points, :].T for x0 in firsts]
    for e in range(2):
        for q in range(points):
            kb[e, q] = jnp.broadcast_to(kts[e][:, q : q + 1], (ys, cols))
    faces = []
    for e in range(2):
        for i in range(parts):
            for c in pieces[e, i]:
                c.wait()
            for q in range(i * size, (i + 1) * size):
                edge[e, q] = kerr_column(src[e, q], fld[e, q], kb[e, q])
        rows_of[e].wait()
        rows = []
        for b in range(ly):
            rhs = edge[e, :, b * points : (b + 1) * points, :].reshape(pts, cols)
            rows.append(matmul(ops[e, b], rhs))
        faces.append(jnp.concatenate(rows, axis=0).astype(bf16))
    left, right = faces
    msg[0:ys, :] = jnp.where(is_a, right, left)
    msg[ys : 2 * ys, :] = jnp.where(is_a, left, right)
    matrix.wait()
    x_map = jnp.where(is_a, own[...], own[...].T).astype(bf16)
    msg[2 * ys :, :] = jnp.concatenate([x_map[: ys // 2], x_map[ys // 2 :]], axis=1)


def split_message(m, ys):
    packed = m[2 * ys :]
    return m[:ys], m[ys : 2 * ys], jnp.concatenate([packed[:, :ys], packed[:, ys:]], axis=0)


def leaves_body(points, edge, source, field, kerr, leaf_ops, part, ends, rhs_all):
    lx, ly, pts, _ = leaf_ops.shape
    xs, ys, cols = source.shape
    kt = kerr[...].T
    for a in range(lx):
        for q in range(points):
            x = a * points + q
            if a == 0:
                col = edge[0, q]
            elif a == lx - 1:
                col = edge[1, q]
            else:
                col = kerr_column(source[x], field[x], kt[:, x : x + 1])
            rhs_all[x] = col
        for b in range(ly):
            rhs = rhs_all[a * points : (a + 1) * points, b * points : (b + 1) * points, :]
            out = matmul(leaf_ops[a, b], rhs.reshape(pts, cols))
            for q in range(points):
                r = (a * points + q) * ys + b * points
                part[r : r + points, :] = out[q * points : (q + 1) * points, :]
    ends[0:xs, :] = part[pl.ds(0, xs, stride=ys), :]
    ends[xs:, :] = part[pl.ds(ys - 1, xs, stride=ys), :]


def compose_body(count, xs, own, got, msg, keep, inner_map):
    ys = own.shape[1] // 2
    place = lax.axis_index("gx")
    inner = (place == count // 2 - 1) | (place == count // 2)
    f_own, g_own, x_own = split_message(own[...], ys)
    f_got, g_got, x_got = split_message(got[...], ys)
    f_in = jnp.where(inner, f_own, f_got)
    g_in = jnp.where(inner, g_own, g_got)
    x_in = jnp.where(inner, x_own, x_got)
    f_out = jnp.where(inner, f_got, f_own)
    reach = matmul(x_in, f_out) + f_in.astype(f32)
    msg[0:ys, :] = reach.astype(bf16)
    msg[ys:, :] = (f_in.astype(f32) + (lift_weight / xs) * f_out.astype(f32)).astype(bf16)
    keep[0] = f_out.astype(f32)
    keep[1] = g_in.astype(f32)
    keep[2] = reach
    inner_map[...] = x_in


def weights_body(kerr, wave, kerr_b, wave_b):
    xs, ys, cols = kerr_b.shape
    kt, wt = kerr[...].T, wave[...].T
    for x in range(xs):
        kerr_b[x] = jnp.broadcast_to(kt[:, x : x + 1], (ys, cols))
        wave_b[x] = jnp.broadcast_to(wt[:, x : x + 1], (ys, cols))


def profiles(xs):
    i = lax.broadcasted_iota(jnp.int32, (xs, 1), 0).astype(f32)
    return (xs - i) / xs, (i + 1.0) / xs


def edge_columns(ends, w, z, pair, cross):
    xs = pair.shape[0]
    ys = w.shape[0]
    lp, rp = profiles(xs)
    low = ends[0:xs, :] + (lp * w[0:1, :] + rp * z[0:1, :])
    high = ends[xs:, :] + (lp * w[ys - 1 : ys, :] + rp * z[ys - 1 : ys, :])
    even = lax.axis_index("gy") % 2 == 0
    pair[...] = jnp.where(even, high, low).astype(bf16)
    cross[...] = jnp.where(even, low, high).astype(bf16)


def finish_body(count, got, keep, inner_map, ends, waves, halo, pair, cross):
    ys = got.shape[0] // 2
    xs = pair.shape[0]
    place = lax.axis_index("gx")
    inner = (place == count // 2 - 1) | (place == count // 2)
    is_a = place < count // 2
    back = got[0:ys, :]
    e_got = got[ys:, :].astype(f32)
    f_out, g_in, reach = keep[0], keep[1], keep[2]
    t = lax.dot_general(
        inner_map[...], back, (((0,), (0,)), ((), ())), preferred_element_type=f32
    ) + g_in
    back = back.astype(f32)
    forward = jnp.where(inner, f_out, 0.0)
    backward = jnp.where(inner, back, t)
    w = lift_weight * jnp.where(is_a, forward, backward)
    z = lift_weight * jnp.where(is_a, backward, forward)
    waves[0] = w
    waves[1] = z
    toward = jnp.where(
        inner,
        e_got + lift_weight * reach,
        g_in + lift_weight * (f_out + back * (1.0 / xs)),
    )
    away = jnp.where(inner, f_out + lift_weight * t, 0.0)
    halo[0] = jnp.where(is_a, away, toward).astype(bf16)
    halo[1] = jnp.where(is_a, toward, away).astype(bf16)
    edge_columns(ends, w, z, pair, cross)


def ends_body(ends, waves, pair, cross):
    edge_columns(ends, waves[0], waves[1], pair, cross)


def stencil(group, ys):
    shape = (group * ys, (group + 2) * ys)
    i = lax.broadcasted_iota(jnp.int32, shape, 0)
    j = lax.broadcasted_iota(jnp.int32, shape, 1)
    away = abs(i // ys + 1 - j // ys) + abs(i % ys - j % ys)
    return jnp.where(away == 0, -4.0, jnp.where(away == 1, 1.0, 0.0)).astype(bf16)


def update_body(
    strip, group, chunk, last, part, waves, halo, kerr_b, wave_b, source, updated, residual,
    strips, late, u, res, sems,
):
    xs, ys, cols = source.shape
    w, z = waves[0], waves[1]
    u[0] = halo[0]
    u[xs + 1] = halo[1]
    taps = stencil(group, ys)
    inside = pl.ds(strip, ys - 2 * strip)
    copies = []

    def send(src, dst):
        copies.append(pltpu.make_async_copy(src, dst, sems.at[len(copies)]))
        copies[-1].start()

    def lift(x):
        lp, rp = (xs - x) / xs, (x + 1) / xs
        u[x + 1] = (part[x * ys : (x + 1) * ys, :] + (lp * w + rp * z)).astype(bf16)
        if (x + 1) % chunk == 0:
            at = pl.ds(x + 1 - chunk, chunk)
            send(u.at[pl.ds(x + 2 - chunk, chunk)], updated.at[at])

    def residue(x):
        near = matmul(taps, u[x : x + group + 2].reshape((group + 2) * ys, cols))
        for q in range(group):
            m = u[x + q + 1].astype(f32)
            s = source[x + q].astype(f32)
            r = near[q * ys : (q + 1) * ys] + (m * (wave_b[x + q] + kerr_b[x + q] * (m * m)) - s)
            strips[0, x + q] = r[:strip, :]
            strips[1, x + q] = r[ys - strip :, :]
            mid = r[strip : ys - strip, :].astype(bf16)
            if x >= xs - last:
                late[x + q - (xs - last)] = mid
            else:
                res[x + q] = mid
        end = x + group
        if end % chunk == 0 and end <= xs - last:
            at = pl.ds(end - chunk, chunk)
            send(res.at[at], residual.at[at, inside])

    ahead = 64
    for x in range(xs + ahead):
        if x < xs:
            lift(x)
        if x >= ahead and (x - ahead) % group == 0:
            residue(x - ahead)
    for c in copies:
        c.wait()


def seam_body(count, strip, last, strips, late, pair, cross, _, residual, work, out, sems):
    xs, ys, cols = residual.shape
    copies = [
        pltpu.make_async_copy(
            late,
            residual.at[pl.ds(xs - last, last), pl.ds(strip, ys - 2 * strip)],
            sems.at[2],
        )
    ]
    copies[0].start()
    g = lax.axis_index("gy")
    even = g % 2 == 0
    zero = jnp.zeros((), f32)
    p, c = pair[...].astype(f32), cross[...].astype(f32)
    low = jnp.where(g == 0, zero, jnp.where(even, c, p))
    high = jnp.where(g == count - 1, zero, jnp.where(even, p, c))
    for e, (row, add) in enumerate(((0, low), (strip - 1, high))):
        work[e] = strips[e].reshape(xs * strip, cols)
        at = pl.ds(row, xs, stride=strip)
        work[e, at, :] = work[e, at, :] + add
        out[e] = work[e].reshape(xs, strip, cols).astype(bf16)
        y0 = 0 if e == 0 else ys - strip
        copies.append(
            pltpu.make_async_copy(out.at[e], residual.at[:, pl.ds(y0, strip), :], sems.at[e])
        )
        copies[-1].start()
    for c in copies:
        c.wait()


def gathered_sweeps(message, ys, xs, count):
    place = lax.axis_index("gx")
    every = lax.all_gather(message, "gx").astype(f32)
    right, left = every[:, :ys], every[:, ys : 2 * ys]
    packed = every[:, 2 * ys :]
    maps = jnp.concatenate([packed[:, :, :ys], packed[:, :, ys:]], axis=1)
    start = jnp.zeros_like(right[0])
    exact = functools.partial(jnp.dot, precision=lax.Precision.HIGHEST)

    def up(state, inp):
        return exact(inp[0], state) + inp[1], state

    def down(state, inp):
        return exact(inp[0].T, state) + inp[1], state

    _, w = lax.scan(up, start, (maps, right))
    _, z = lax.scan(down, start, (maps, left), reverse=True)
    before, after = jnp.maximum(place - 1, 0), jnp.minimum(place + 1, count - 1)
    low = right[before] + lift_weight * (w[before] / xs + z[before])
    high = left[after] + lift_weight * (w[after] + z[after] / xs)
    low = jnp.where(place == 0, 0.0, low)
    high = jnp.where(place == count - 1, 0.0, high)
    return lift_weight * jnp.stack([w[place], z[place]]), jnp.stack([low, high]).astype(bf16)


def per_device(source, field, kerr, wave, leaf_ops, transfer_ops):
    xs, ys, cols = source.shape
    lx, ly, pts, _ = leaf_ops.shape
    points = xs // lx
    n_gx, n_gy = lax.axis_size("gx"), lax.axis_size("gy")
    doubling = n_gx == 4
    shape = jax.ShapeDtypeStruct
    dots = 2 * lx * ly * pts * pts * cols

    message, edge = call(
        functools.partial(faces_body, n_gx // 2 if doubling else n_gx, points, 1),
        (shape((2 * ys + ys // 2, cols), bf16), shape((2, points, ys, cols), bf16)),
        [HBM] * 5,
        scratch=[
            pltpu.VMEM((2, points, ys, cols), bf16),
            pltpu.VMEM((2, points, ys, cols), bf16),
            pltpu.VMEM((2, ly, points, pts), bf16),
            pltpu.VMEM((xs, ys), f32),
            pltpu.VMEM((ys, ys), f32),
            pltpu.VMEM((2, points, ys, cols), f32),
            pltpu.SemaphoreType.DMA((2, 8)),
            pltpu.SemaphoreType.DMA((4,)),
        ],
        cost=(dots // 8, 2 << 20),
    )(*map(in_hbm, (source, field, kerr, leaf_ops, transfer_ops)))
    message, edge, source, field, kerr, wave, leaf_ops = lax.optimization_barrier(
        (message, edge, source, field, kerr, wave, leaf_ops)
    )

    if doubling:
        other = lax.ppermute(message, "gx", [(i, i ^ 1) for i in range(n_gx)])

    part, ends = call(
        functools.partial(leaves_body, points),
        (shape((xs * ys, cols), f32), shape((2 * xs, cols), f32)),
        [VMEM] * 5,
        scratch=[pltpu.VMEM((xs, ys, cols), bf16)],
        cost=(dots, 6 << 20),
    )(edge, source, field, kerr, leaf_ops)

    kerr_b, wave_b = call(
        weights_body,
        (shape((xs, ys, cols), f32), shape((xs, ys, cols), f32)),
        [VMEM] * 2,
        cost=(xs * ys * cols, 4 << 20),
    )(kerr, wave)

    column = shape((xs, cols), bf16)
    if doubling:
        other, part, ends = lax.optimization_barrier((other, part, ends))
        reach, keep, inner_map = call(
            functools.partial(compose_body, n_gx, xs),
            (shape((2 * ys, cols), bf16), shape((3, ys, cols), f32), shape((ys, ys), bf16)),
            [VMEM] * 2,
        )(message, other)
        far = lax.ppermute(reach, "gx", [(i, i ^ 2) for i in range(n_gx)])
        far, kerr_b, wave_b = lax.optimization_barrier((far, kerr_b, wave_b))
        waves, halo, pair, cross = call(
            functools.partial(finish_body, n_gx),
            (shape((2, ys, cols), f32), shape((2, ys, cols), bf16), column, column),
            [VMEM] * 4,
        )(far, keep, inner_map, ends)
    else:
        waves, halo = gathered_sweeps(message, ys, xs, n_gx)
        pair, cross = call(ends_body, (column, column), [VMEM] * 2)(ends, waves)

    pair_to = [(i, i + 1 - 2 * (i % 2)) for i in range(n_gy)]
    cross_to = [(i, (i - 1 + 2 * (i % 2)) % n_gy) for i in range(n_gy)]
    pair = lax.ppermute(pair, "gy", pair_to)
    cross = lax.ppermute(cross, "gy", cross_to)

    strip, group, chunk, last = 16, 2, xs // 4, xs // 2
    big = shape((xs, ys, cols), bf16)
    updated, residual, strips, late = call(
        functools.partial(update_body, strip, group, chunk, last),
        (
            big,
            big,
            shape((2, xs, strip, cols), f32),
            shape((last, ys - 2 * strip, cols), bf16),
        ),
        [VMEM] * 6,
        out_specs=(ANY, ANY, VMEM, VMEM),
        scratch=[
            pltpu.VMEM((xs + 2, ys, cols), bf16),
            pltpu.VMEM((xs, ys - 2 * strip, cols), bf16),
            pltpu.SemaphoreType.DMA((2 * xs // chunk,)),
        ],
        cost=(20 * xs * ys * cols, 10 << 20),
    )(part, waves, halo, kerr_b, wave_b, source)

    residual = call(
        functools.partial(seam_body, n_gy, strip, last),
        big,
        [VMEM] * 4 + [ANY],
        out_specs=ANY,
        scratch=[
            pltpu.VMEM((2, xs * strip, cols), f32),
            pltpu.VMEM((2, xs, strip, cols), bf16),
            pltpu.SemaphoreType.DMA((3,)),
        ],
        aliases={4: 0},
    )(strips, late, pair, cross, residual)
    return updated, residual


def solution(mesh):
    return jax.shard_map(
        per_device,
        mesh=mesh,
        in_specs=(
            P(("grp", "gx"), "gy", None),
            P(("grp", "gx"), "gy", None),
            P(("grp", "gx"), "gy"),
            P(("grp", "gx"), "gy"),
            P("gx", "gy", None, None),
            P("gx", "gy", None),
        ),
        out_specs=(P(("grp", "gx"), "gy", None), P(("grp", "gx"), "gy", None)),
        check_vma=False,
    )
```

```python
import functools

import jax
import jax.numpy as jnp
from jax import lax
from jax.experimental import pallas as pl
from jax.experimental.pallas import tpu as pltpu
from jax.sharding import PartitionSpec as P

lift_weight = 0.3
f32, bf16 = jnp.float32, jnp.bfloat16
VMEM = pl.BlockSpec(memory_space=pltpu.VMEM)
ANY = pl.BlockSpec(memory_space=pl.ANY)
HBM = pl.BlockSpec(memory_space=pltpu.HBM)


def call(body, outs, ins, out_specs=None, scratch=(), cost=(0, 0), aliases=None):
    def run(*args):
        return pl.pallas_call(
            body,
            out_shape=outs,
            in_specs=ins,
            out_specs=out_specs if out_specs is not None else jax.tree.map(lambda _: VMEM, outs),
            scratch_shapes=scratch,
            input_output_aliases=aliases or {},
            compiler_params=pltpu.CompilerParams(vmem_limit_bytes=24 << 20),
            cost_estimate=pl.CostEstimate(
                flops=cost[0], bytes_accessed=cost[1], transcendentals=0
            ),
        )(*args)

    return run


def in_hbm(x):
    return pltpu.with_memory_space_constraint(x, pltpu.HBM)


def matmul(a, b):
    return jnp.dot(a, b, preferred_element_type=f32)


def kerr_column(source, field, kerr):
    s, f = source.astype(f32), field.astype(f32)
    return (s - kerr * f * f * f).astype(bf16)


def seat(paired):
    if not paired:
        return True, True
    place = lax.axis_index("gx")
    return place < 2, (place == 1) | (place == 2)


def faces_body(
    paired, points, parts, source, field, kerr_all, leaf_ops, transfer, far, near, edge, src, fld, ops,
    kerr, own, kb, sems, more,
):
    lx, ly, pts, _ = leaf_ops.shape
    xs, ys, cols = source.shape
    copy = pltpu.make_async_copy
    firsts = (0, xs - points)
    size = points // parts
    coef = copy(kerr_all, kerr, more.at[0])
    coef.start()
    pieces = {}
    for e, x0 in enumerate(firsts):
        for i in range(parts):
            at, here = pl.ds(x0 + i * size, size), pl.ds(i * size, size)
            pieces[e, i] = (
                copy(source.at[at], src.at[e, here], sems.at[e, 2 * i]),
                copy(field.at[at], fld.at[e, here], sems.at[e, 2 * i + 1]),
            )
            for c in pieces[e, i]:
                c.start(priority=e)
    rows_of = []
    for e, (a, r0) in enumerate(((0, 0), (lx - 1, pts - points))):
        rows_of.append(copy(leaf_ops.at[a, :, pl.ds(r0, points), :], ops.at[e], more.at[2 + e]))
        rows_of[e].start()
    matrix = copy(transfer.at[0], own, more.at[1])
    matrix.start()
    is_a, inner = seat(paired)
    coef.wait()
    kts = [kerr[x0 : x0 + points, :].T for x0 in firsts]
    for e in range(2):
        for q in range(points):
            kb[e, q] = jnp.broadcast_to(kts[e][:, q : q + 1], (ys, cols))
    faces = []
    for e in range(2):
        for i in range(parts):
            for c in pieces[e, i]:
                c.wait()
            for q in range(i * size, (i + 1) * size):
                edge[e, q] = kerr_column(src[e, q], fld[e, q], kb[e, q])
        rows_of[e].wait()
        rows = []
        for b in range(ly):
            rhs = edge[e, :, b * points : (b + 1) * points, :].reshape(pts, cols)
            rows.append(matmul(ops[e, b], rhs))
        faces.append(jnp.concatenate(rows, axis=0).astype(bf16))
    left, right = faces
    toward = jnp.where(is_a, right, left)
    far[0:ys, :] = toward
    near[0:ys, :] = jnp.where(inner, jnp.where(is_a, left, right), toward)
    matrix.wait()
    x_map = jnp.where(is_a, own[...], own[...].T).astype(bf16)
    x_map = jnp.concatenate([x_map[: ys // 2], x_map[ys // 2 :]], axis=1)
    far[ys:, :] = x_map
    near[ys:, :] = x_map


def unpack(message):
    cols = message.shape[1]
    ys = 2 * message.shape[0] // 3
    packed = message[ys:]
    half = cols // 2
    return message[:ys], jnp.concatenate([packed[:, :half], packed[:, half:]], axis=0)


def leaves_body(
    points, edge, source, field, kerr, leaf_ops, part, ends, mid, fld, rhs_all, sems
):
    lx, ly, pts, _ = leaf_ops.shape
    xs, ys, cols = source.shape
    inner = pl.ds(points, xs - 2 * points)
    copies = [
        pltpu.make_async_copy(source.at[inner], mid, sems.at[0]),
        pltpu.make_async_copy(field.at[inner], fld, sems.at[1]),
    ]
    for c in copies:
        c.start()

    def leaf_row(a, rows):
        for b in range(ly):
            rhs = rows[:, b * points : (b + 1) * points, :].reshape(pts, cols)
            out = matmul(leaf_ops[a, b], rhs)
            for q in range(points):
                r = (a * points + q) * ys + b * points
                part[r : r + points, :] = out[q * points : (q + 1) * points, :]

    leaf_row(0, edge.at[0])
    leaf_row(lx - 1, edge.at[1])
    kt = kerr[...].T
    for c in copies:
        c.wait()
    for a in range(1, lx - 1):
        for q in range(points):
            x, r = a * points + q, (a - 1) * points + q
            rhs_all[r] = kerr_column(mid[r], fld[r], kt[:, x : x + 1])
        leaf_row(a, rhs_all.at[pl.ds((a - 1) * points, points)])
    ends[0:xs, :] = part[pl.ds(0, xs, stride=ys), :]
    ends[xs:, :] = part[pl.ds(ys - 1, xs, stride=ys), :]


def weights_body(kerr, wave, kerr_b, wave_b):
    xs, ys, cols = kerr_b.shape
    kt, wt = kerr[...].T, wave[...].T
    for x in range(xs):
        kerr_b[x] = jnp.broadcast_to(kt[:, x : x + 1], (ys, cols))
        wave_b[x] = jnp.broadcast_to(wt[:, x : x + 1], (ys, cols))


def profiles(xs):
    i = lax.broadcasted_iota(jnp.int32, (xs, 1), 0).astype(f32)
    return (xs - i) / xs, (i + 1.0) / xs


def edge_columns(ends, w, z, pair, cross):
    xs = pair.shape[0]
    ys = w.shape[0]
    lp, rp = profiles(xs)
    low = ends[0:xs, :] + (lp * w[0:1, :] + rp * z[0:1, :])
    high = ends[xs:, :] + (lp * w[ys - 1 : ys, :] + rp * z[ys - 1 : ys, :])
    even = lax.axis_index("gy") % 2 == 0
    pair[...] = jnp.where(even, high, low).astype(bf16)
    cross[...] = jnp.where(even, low, high).astype(bf16)


def finish_body(far, near, got_1, got_2, got_3, ends, waves, halo, pair, cross):
    xs = pair.shape[0]
    is_a, inner = seat(True)
    own_face, own_map = unpack(far[...])
    own_near, _ = unpack(near[...])
    mate_face, mate_map = unpack(got_1[...])
    face_2, map_2 = unpack(got_2[...])
    face_3, map_3 = unpack(got_3[...])
    other_map = jnp.where(inner, map_3, map_2)
    other_in = jnp.where(inner, face_3, face_2).astype(f32)
    other_out = jnp.where(inner, face_2, face_3)
    back_in = matmul(other_map, other_out) + other_in
    in_map = jnp.where(inner, own_map, mate_map)
    out_face = jnp.where(inner, mate_face, own_face)
    in_back = jnp.where(inner, own_near, mate_face).astype(f32)
    reach = matmul(in_map, out_face) + own_face.astype(f32)
    back_out = in_back + lax.dot_general(
        in_map, back_in.astype(bf16), (((0,), (0,)), ((), ())), preferred_element_type=f32
    )
    out_face, other_out = out_face.astype(f32), other_out.astype(f32)
    ahead = jnp.where(inner, out_face, 0.0)
    back = jnp.where(inner, back_in, back_out)
    w = lift_weight * jnp.where(is_a, ahead, back)
    z = lift_weight * jnp.where(is_a, back, ahead)
    waves[0] = w
    waves[1] = z
    edge_columns(ends, w, z, pair, cross)
    toward = jnp.where(
        inner,
        other_in + lift_weight * (reach + other_out * (1.0 / xs)),
        in_back + lift_weight * (out_face + back_in * (1.0 / xs)),
    )
    away = jnp.where(inner, out_face + lift_weight * back_out, 0.0)
    halo[0] = jnp.where(is_a, away, toward).astype(bf16)
    halo[1] = jnp.where(is_a, toward, away).astype(bf16)


def ends_body(ends, waves, pair, cross):
    edge_columns(ends, waves[0], waves[1], pair, cross)


def stencil(group, ys):
    shape = (group * ys, (group + 2) * ys)
    i = lax.broadcasted_iota(jnp.int32, shape, 0)
    j = lax.broadcasted_iota(jnp.int32, shape, 1)
    away = abs(i // ys + 1 - j // ys) + abs(i % ys - j % ys)
    return jnp.where(away == 0, -4.0, jnp.where(away == 1, 1.0, 0.0)).astype(bf16)


def update_body(
    strip, group, chunk, last, part, waves, halo, kerr_b, wave_b, src, mid, updated, residual,
    strips, late, u, res, sems,
):
    xs, ys, cols = updated.shape
    points = src.shape[1]

    def source(x):
        if x < points:
            return src[0, x]
        return src[1, x - xs + points] if x >= xs - points else mid[x - points]

    w, z = waves[0], waves[1]
    u[0] = halo[0]
    u[xs + 1] = halo[1]
    taps = stencil(group, ys)
    inside = pl.ds(strip, ys - 2 * strip)
    copies = []

    def send(src, dst):
        copies.append(pltpu.make_async_copy(src, dst, sems.at[len(copies)]))
        copies[-1].start()

    def lift(x, rise):
        u[x + 1] = (part[x * ys : (x + 1) * ys, :] + rise).astype(bf16)
        if (x + 1) % chunk == 0:
            at = pl.ds(x + 1 - chunk, chunk)
            send(u.at[pl.ds(x + 2 - chunk, chunk)], updated.at[at])

    def residue(x):
        near = matmul(taps, u[x : x + group + 2].reshape((group + 2) * ys, cols))
        for q in range(group):
            m = u[x + q + 1].astype(f32)
            s = source(x + q).astype(f32)
            r = near[q * ys : (q + 1) * ys] + (m * (wave_b[x + q] + kerr_b[x + q] * (m * m)) - s)
            strips[0, x + q] = r[:strip, :]
            strips[1, x + q] = r[ys - strip :, :]
            mid = r[strip : ys - strip, :].astype(bf16)
            if x >= xs - last:
                late[x + q - (xs - last)] = mid
            else:
                res[x + q] = mid
        end = x + group
        if end % chunk == 0 and end <= xs - last:
            at = pl.ds(end - chunk, chunk)
            send(res.at[at], residual.at[at, inside])

    ahead = 64
    rise, slope = w + z * (1.0 / xs), (z - w) * (1.0 / xs)
    for x in range(xs + ahead):
        if x < xs:
            lift(x, rise)
            rise = rise + slope
        if x >= ahead and (x - ahead) % group == 0:
            residue(x - ahead)
    for c in copies:
        c.wait()


def seam_body(count, strip, last, strips, late, pair, cross, _, residual, work, out, sems):
    xs, ys, cols = residual.shape
    copies = [
        pltpu.make_async_copy(
            late,
            residual.at[pl.ds(xs - last, last), pl.ds(strip, ys - 2 * strip)],
            sems.at[2],
        )
    ]
    copies[0].start()
    g = lax.axis_index("gy")
    even = g % 2 == 0
    zero = jnp.zeros((), f32)
    p, c = pair[...].astype(f32), cross[...].astype(f32)
    low = jnp.where(g == 0, zero, jnp.where(even, c, p))
    high = jnp.where(g == count - 1, zero, jnp.where(even, p, c))
    for e, (row, add) in enumerate(((0, low), (strip - 1, high))):
        work[e] = strips[e].reshape(xs * strip, cols)
        at = pl.ds(row, xs, stride=strip)
        work[e, at, :] = work[e, at, :] + add
        out[e] = work[e].reshape(xs, strip, cols).astype(bf16)
        y0 = 0 if e == 0 else ys - strip
        copies.append(
            pltpu.make_async_copy(out.at[e], residual.at[:, pl.ds(y0, strip), :], sems.at[e])
        )
        copies[-1].start()
    for c in copies:
        c.wait()


def gathered_sweeps(far, near, ys, xs, count):
    place = lax.axis_index("gx")
    every, left = (lax.all_gather(m, "gx").astype(f32) for m in (far, near))
    right, left = every[:, :ys], left[:, :ys]
    half = every.shape[2] // 2
    maps = jnp.concatenate([every[:, ys:, :half], every[:, ys:, half:]], axis=1)
    start = jnp.zeros_like(right[0])
    exact = functools.partial(jnp.dot, precision=lax.Precision.HIGHEST)

    def up(state, inp):
        return exact(inp[0], state) + inp[1], state

    def down(state, inp):
        return exact(inp[0].T, state) + inp[1], state

    _, w = lax.scan(up, start, (maps, right))
    _, z = lax.scan(down, start, (maps, left), reverse=True)
    before, after = jnp.maximum(place - 1, 0), jnp.minimum(place + 1, count - 1)
    low = right[before] + lift_weight * (w[before] / xs + z[before])
    high = left[after] + lift_weight * (w[after] + z[after] / xs)
    low = jnp.where(place == 0, 0.0, low)
    high = jnp.where(place == count - 1, 0.0, high)
    return lift_weight * jnp.stack([w[place], z[place]]), jnp.stack([low, high]).astype(bf16)


def per_device(source, field, kerr, wave, leaf_ops, transfer_ops):
    xs, ys, cols = source.shape
    lx, ly, pts, _ = leaf_ops.shape
    points = xs // lx
    n_gx, n_gy = lax.axis_size("gx"), lax.axis_size("gy")
    paired = n_gx == 4
    shape = jax.ShapeDtypeStruct
    dots = 2 * lx * ly * pts * pts * cols

    edges = shape((2, points, ys, cols), bf16)
    edges = shape((2, points, ys, cols), bf16)
    message = shape((ys + ys // 2, cols), bf16)
    far, near, edge, src = call(
        functools.partial(faces_body, paired, points, 1),
        (message, message, edges, edges),
        [HBM] * 5,
        scratch=[
            pltpu.VMEM((2, points, ys, cols), bf16),
            pltpu.VMEM((2, ly, points, pts), bf16),
            pltpu.VMEM((xs, ys), f32),
            pltpu.VMEM((ys, ys), f32),
            pltpu.VMEM((2, points, ys, cols), f32),
            pltpu.SemaphoreType.DMA((2, 2)),
            pltpu.SemaphoreType.DMA((4,)),
        ],
        cost=(dots // 8, 2 << 20),
    )(*map(in_hbm, (source, field, kerr, leaf_ops, transfer_ops)))
    far, near, edge, source, field, kerr, wave, leaf_ops = lax.optimization_barrier(
        (far, near, edge, source, field, kerr, wave, leaf_ops)
    )

    if paired:
        sent = [(2, far), (3, far), (1, near)]
        got = [lax.ppermute(m, "gx", [(i, i ^ k) for i in range(n_gx)]) for k, m in sent]

    between = shape((xs - 2 * points, ys, cols), bf16)
    part, ends, mid = call(
        functools.partial(leaves_body, points),
        (shape((xs * ys, cols), f32), shape((2 * xs, cols), f32), between),
        [VMEM, HBM, HBM, VMEM, VMEM],
        scratch=[
            pltpu.VMEM(between.shape, bf16),
            pltpu.VMEM(between.shape, bf16),
            pltpu.SemaphoreType.DMA((2,)),
        ],
        cost=(dots, 6 << 20),
    )(edge, in_hbm(source), in_hbm(field), kerr, leaf_ops)

    kerr_b, wave_b = call(
        weights_body,
        (shape((xs, ys, cols), f32), shape((xs, ys, cols), f32)),
        [VMEM] * 2,
        cost=(xs * ys * cols, 4 << 20),
    )(kerr, wave)

    column = shape((xs, cols), bf16)
    if paired:
        *got, part, ends, kerr_b, wave_b = lax.optimization_barrier(
            (*got, part, ends, kerr_b, wave_b)
        )
        waves, halo, pair, cross = call(
            finish_body,
            (shape((2, ys, cols), f32), shape((2, ys, cols), bf16), column, column),
            [VMEM] * 6,
        )(far, near, got[2], got[0], got[1], ends)
    else:
        waves, halo = gathered_sweeps(far, near, ys, xs, n_gx)
        pair, cross = call(ends_body, (column, column), [VMEM] * 2)(ends, waves)

    pair_to = [(i, i + 1 - 2 * (i % 2)) for i in range(n_gy)]
    cross_to = [(i, (i - 1 + 2 * (i % 2)) % n_gy) for i in range(n_gy)]
    pair = lax.ppermute(pair, "gy", pair_to)
    cross = lax.ppermute(cross, "gy", cross_to)

    strip, group, chunk, last = 16, 2, xs // 4, xs // 2
    big = shape((xs, ys, cols), bf16)
    updated, residual, strips, late = call(
        functools.partial(update_body, strip, group, chunk, last),
        (
            big,
            big,
            shape((2, xs, strip, cols), f32),
            shape((last, ys - 2 * strip, cols), bf16),
        ),
        [VMEM] * 7,
        out_specs=(ANY, ANY, VMEM, VMEM),
        scratch=[
            pltpu.VMEM((xs + 2, ys, cols), bf16),
            pltpu.VMEM((xs, ys - 2 * strip, cols), bf16),
            pltpu.SemaphoreType.DMA((2 * xs // chunk,)),
        ],
        cost=(20 * xs * ys * cols, 10 << 20),
    )(part, waves, halo, kerr_b, wave_b, src, mid)

    residual = call(
        functools.partial(seam_body, n_gy, strip, last),
        big,
        [VMEM] * 4 + [ANY],
        out_specs=ANY,
        scratch=[
            pltpu.VMEM((2, xs * strip, cols), f32),
            pltpu.VMEM((2, xs, strip, cols), bf16),
            pltpu.SemaphoreType.DMA((3,)),
        ],
        aliases={4: 0},
    )(strips, late, pair, cross, residual)
    return updated, residual


def solution(mesh):
    return jax.shard_map(
        per_device,
        mesh=mesh,
        in_specs=(
            P(("grp", "gx"), "gy", None),
            P(("grp", "gx"), "gy", None),
            P(("grp", "gx"), "gy"),
            P(("grp", "gx"), "gy"),
            P("gx", "gy", None, None),
            P("gx", "gy", None),
        ),
        out_specs=(P(("grp", "gx"), "gy", None), P(("grp", "gx"), "gy", None)),
        check_vma=False,
    )
```

```python
import functools

import jax
import jax.numpy as jnp
from jax import lax
from jax.experimental import pallas as pl
from jax.experimental.pallas import tpu as pltpu
from jax.sharding import PartitionSpec as P

lift_weight = 0.3
f32, bf16 = jnp.float32, jnp.bfloat16
VMEM = pl.BlockSpec(memory_space=pltpu.VMEM)
ANY = pl.BlockSpec(memory_space=pl.ANY)
HBM = pl.BlockSpec(memory_space=pltpu.HBM)


def call(body, outs, ins, out_specs=None, scratch=(), cost=(0, 0), aliases=None):
    def run(*args):
        return pl.pallas_call(
            body,
            out_shape=outs,
            in_specs=ins,
            out_specs=out_specs if out_specs is not None else jax.tree.map(lambda _: VMEM, outs),
            scratch_shapes=scratch,
            input_output_aliases=aliases or {},
            compiler_params=pltpu.CompilerParams(vmem_limit_bytes=24 << 20),
            cost_estimate=pl.CostEstimate(
                flops=cost[0], bytes_accessed=cost[1], transcendentals=0
            ),
        )(*args)

    return run


def in_hbm(x):
    return pltpu.with_memory_space_constraint(x, pltpu.HBM)


def matmul(a, b):
    return jnp.dot(a, b, preferred_element_type=f32)


def kerr_column(source, field, kerr):
    s, f = source.astype(f32), field.astype(f32)
    return (s - kerr * f * f * f).astype(bf16)


def seat(paired):
    if not paired:
        return True, True
    place = lax.axis_index("gx")
    return place < 2, (place == 1) | (place == 2)


def faces_body(
    paired, points, parts, source, field, kerr_all, leaf_ops, transfer, far, near, edge, src, kb, fld,
    ops, kerr, own, sems, more,
):
    lx, ly, pts, _ = leaf_ops.shape
    xs, ys, cols = source.shape
    copy = pltpu.make_async_copy
    firsts = (0, xs - points)
    size = points // parts
    coef = copy(kerr_all, kerr, more.at[0])
    coef.start()
    matrix = copy(transfer.at[0], own, more.at[1])
    matrix.start()
    pieces = {}
    for e, x0 in enumerate(firsts):
        for i in range(parts):
            at, here = pl.ds(x0 + i * size, size), pl.ds(i * size, size)
            pieces[e, i] = (
                copy(source.at[at], src.at[e, here], sems.at[e, 2 * i]),
                copy(field.at[at], fld.at[e, here], sems.at[e, 2 * i + 1]),
            )
            for c in pieces[e, i]:
                c.start()
    rows_of = []
    for e, (a, r0) in enumerate(((0, 0), (lx - 1, pts - points))):
        rows_of.append(copy(leaf_ops.at[a, :, pl.ds(r0, points), :], ops.at[e], more.at[2 + e]))
        rows_of[e].start()
    is_a, inner = seat(paired)
    coef.wait()
    kts = [kerr[x0 : x0 + points, :].T for x0 in firsts]
    for e in range(2):
        for q in range(points):
            kb[e, q] = jnp.broadcast_to(kts[e][:, q : q + 1], (ys, cols))
    matrix.wait()
    x_map = jnp.where(is_a, own[...], own[...].T).astype(bf16)
    x_map = jnp.concatenate([x_map[: ys // 2], x_map[ys // 2 :]], axis=1)
    far[ys:, :] = x_map
    near[ys:, :] = x_map
    faces = []
    for e in range(2):
        for i in range(parts):
            for c in pieces[e, i]:
                c.wait()
            for q in range(i * size, (i + 1) * size):
                edge[e, q] = kerr_column(src[e, q], fld[e, q], kb[e, q])
        rows_of[e].wait()
        rows = []
        for b in range(ly):
            rhs = edge[e, :, b * points : (b + 1) * points, :].reshape(pts, cols)
            rows.append(matmul(ops[e, b], rhs))
        faces.append(jnp.concatenate(rows, axis=0).astype(bf16))
    left, right = faces
    toward = jnp.where(is_a, right, left)
    far[0:ys, :] = toward
    near[0:ys, :] = jnp.where(inner, jnp.where(is_a, left, right), toward)


def unpack(message):
    cols = message.shape[1]
    ys = 2 * message.shape[0] // 3
    packed = message[ys:]
    half = cols // 2
    return message[:ys], jnp.concatenate([packed[:, :half], packed[:, half:]], axis=0)


def leaves_body(
    points, edge, source, field, kerr, wave, leaf_ops, part, ends, mid, kerr_b, wave_b,
    fld, rhs, ops, coef, sems
):
    lx, ly, pts, _ = leaf_ops.shape
    xs, ys, cols = source.shape
    inner = pl.ds(points, xs - 2 * points)
    copy = pltpu.make_async_copy
    coefs = [copy(kerr, coef.at[0], sems.at[0]), copy(wave, coef.at[1], sems.at[1])]
    order = [0, lx - 1] + list(range(1, lx - 1))
    middle = [copy(source.at[inner], mid, sems.at[2]), copy(field.at[inner], fld, sems.at[3])]
    leaves = [copy(leaf_ops.at[a], ops.at[a], sems.at[4 + a]) for a in range(lx)]
    for c in coefs + [leaves[0], leaves[lx - 1]] + middle + leaves[1 : lx - 1]:
        c.start()

    def leaf_row(a, rows):
        leaves[a].wait()
        for b in range(ly):
            column = rows[:, b * points : (b + 1) * points, :].reshape(pts, cols)
            out = matmul(ops[a, b], column)
            for q in range(points):
                r = (a * points + q) * ys + b * points
                part[r : r + points, :] = out[q * points : (q + 1) * points, :]

    for c in coefs:
        c.wait()
    kt, wt = coef[0].T, coef[1].T
    for x in range(xs):
        wave_b[x] = jnp.broadcast_to(wt[:, x : x + 1], (ys, cols))
        if points <= x < xs - points:
            kerr_b[x - points] = jnp.broadcast_to(kt[:, x : x + 1], (ys, cols))
    leaf_row(0, edge.at[0])
    leaf_row(lx - 1, edge.at[1])
    for c in middle:
        c.wait()
    for a in order[2:]:
        for q in range(points):
            r = (a - 1) * points + q
            rhs[r] = kerr_column(mid[r], fld[r], kerr_b[r])
        leaf_row(a, rhs.at[pl.ds((a - 1) * points, points)])
    ends[0:xs, :] = part[pl.ds(0, xs, stride=ys), :]
    ends[xs:, :] = part[pl.ds(ys - 1, xs, stride=ys), :]


def profiles(xs):
    i = lax.broadcasted_iota(jnp.int32, (xs, 1), 0).astype(f32)
    return (xs - i) / xs, (i + 1.0) / xs


def edge_columns(ends, w, z, pair, cross):
    xs = pair.shape[0]
    ys = w.shape[0]
    lp, rp = profiles(xs)
    low = ends[0:xs, :] + (lp * w[0:1, :] + rp * z[0:1, :])
    high = ends[xs:, :] + (lp * w[ys - 1 : ys, :] + rp * z[ys - 1 : ys, :])
    even = lax.axis_index("gy") % 2 == 0
    pair[...] = jnp.where(even, high, low).astype(bf16)
    cross[...] = jnp.where(even, low, high).astype(bf16)


def finish_body(far, near, got_1, got_2, got_3, ends, waves, halo, pair, cross):
    xs = pair.shape[0]
    is_a, inner = seat(True)
    own_face, own_map = unpack(far[...])
    own_near, _ = unpack(near[...])
    mate_face, mate_map = unpack(got_1[...])
    face_2, map_2 = unpack(got_2[...])
    face_3, map_3 = unpack(got_3[...])
    other_map = jnp.where(inner, map_3, map_2)
    other_in = jnp.where(inner, face_3, face_2).astype(f32)
    other_out = jnp.where(inner, face_2, face_3)
    back_in = matmul(other_map, other_out) + other_in
    in_map = jnp.where(inner, own_map, mate_map)
    out_face = jnp.where(inner, mate_face, own_face)
    in_back = jnp.where(inner, own_near, mate_face).astype(f32)
    reach = matmul(in_map, out_face) + own_face.astype(f32)
    back_out = in_back + lax.dot_general(
        in_map, back_in.astype(bf16), (((0,), (0,)), ((), ())), preferred_element_type=f32
    )
    out_face, other_out = out_face.astype(f32), other_out.astype(f32)
    ahead = jnp.where(inner, out_face, 0.0)
    back = jnp.where(inner, back_in, back_out)
    w = lift_weight * jnp.where(is_a, ahead, back)
    z = lift_weight * jnp.where(is_a, back, ahead)
    waves[0] = w
    waves[1] = z
    edge_columns(ends, w, z, pair, cross)
    toward = jnp.where(
        inner,
        other_in + lift_weight * (reach + other_out * (1.0 / xs)),
        in_back + lift_weight * (out_face + back_in * (1.0 / xs)),
    )
    away = jnp.where(inner, out_face + lift_weight * back_out, 0.0)
    halo[0] = jnp.where(is_a, away, toward).astype(bf16)
    halo[1] = jnp.where(is_a, toward, away).astype(bf16)


def ends_body(ends, waves, pair, cross):
    edge_columns(ends, waves[0], waves[1], pair, cross)


def stencil(group, ys):
    shape = (group * ys, (group + 2) * ys)
    i = lax.broadcasted_iota(jnp.int32, shape, 0)
    j = lax.broadcasted_iota(jnp.int32, shape, 1)
    away = abs(i // ys + 1 - j // ys) + abs(i % ys - j % ys)
    return jnp.where(away == 0, -4.0, jnp.where(away == 1, 1.0, 0.0)).astype(bf16)


def update_body(
    strip, group, chunk, last, part, waves, halo, kerr_e, kerr_m, wave_b, src, mid, updated,
    residual, strips, late, u, res, sems,
):
    xs, ys, cols = updated.shape
    points = src.shape[1]

    def row(ends, middle, x):
        if x < points:
            return ends[0, x]
        return ends[1, x - xs + points] if x >= xs - points else middle[x - points]

    w, z = waves[0], waves[1]
    u[0] = halo[0]
    u[xs + 1] = halo[1]
    taps = stencil(group, ys)
    inside = pl.ds(strip, ys - 2 * strip)
    copies = []

    def send(src, dst):
        copies.append(pltpu.make_async_copy(src, dst, sems.at[len(copies)]))
        copies[-1].start()

    def lift(x, rise):
        u[x + 1] = (part[x * ys : (x + 1) * ys, :] + rise).astype(bf16)
        if (x + 1) % chunk == 0:
            at = pl.ds(x + 1 - chunk, chunk)
            send(u.at[pl.ds(x + 2 - chunk, chunk)], updated.at[at])

    def residue(x):
        near = matmul(taps, u[x : x + group + 2].reshape((group + 2) * ys, cols))
        for q in range(group):
            m = u[x + q + 1].astype(f32)
            s = row(src, mid, x + q).astype(f32)
            k = row(kerr_e, kerr_m, x + q)
            r = near[q * ys : (q + 1) * ys] + (m * (wave_b[x + q] + k * (m * m)) - s)
            strips[0, x + q] = r[:strip, :]
            strips[1, x + q] = r[ys - strip :, :]
            body = r[strip : ys - strip, :].astype(bf16)
            if x >= xs - last:
                late[x + q - (xs - last)] = body
            else:
                res[x + q] = body
        end = x + group
        if end % chunk == 0 and end <= xs - last:
            at = pl.ds(end - chunk, chunk)
            send(res.at[at], residual.at[at, inside])

    ahead = xs
    rise, slope = w + z * (1.0 / xs), (z - w) * (1.0 / xs)
    for x in range(xs + ahead):
        if x < xs:
            lift(x, rise)
            rise = rise + slope
        if x >= ahead and (x - ahead) % group == 0:
            residue(x - ahead)
    for c in copies:
        c.wait()


def seam_body(count, strip, last, strips, late, pair, cross, _, residual, work, out, sems):
    xs, ys, cols = residual.shape
    copies = [
        pltpu.make_async_copy(
            late,
            residual.at[pl.ds(xs - last, last), pl.ds(strip, ys - 2 * strip)],
            sems.at[2],
        )
    ]
    copies[0].start()
    g = lax.axis_index("gy")
    even = g % 2 == 0
    zero = jnp.zeros((), f32)
    p, c = pair[...].astype(f32), cross[...].astype(f32)
    low = jnp.where(g == 0, zero, jnp.where(even, c, p))
    high = jnp.where(g == count - 1, zero, jnp.where(even, p, c))
    for e, (row, add) in enumerate(((0, low), (strip - 1, high))):
        work[e] = strips[e].reshape(xs * strip, cols)
        at = pl.ds(row, xs, stride=strip)
        work[e, at, :] = work[e, at, :] + add
        out[e] = work[e].reshape(xs, strip, cols).astype(bf16)
        y0 = 0 if e == 0 else ys - strip
        copies.append(
            pltpu.make_async_copy(out.at[e], residual.at[:, pl.ds(y0, strip), :], sems.at[e])
        )
        copies[-1].start()
    for c in copies:
        c.wait()


def gathered_sweeps(far, near, ys, xs, count):
    place = lax.axis_index("gx")
    every, left = (lax.all_gather(m, "gx").astype(f32) for m in (far, near))
    right, left = every[:, :ys], left[:, :ys]
    half = every.shape[2] // 2
    maps = jnp.concatenate([every[:, ys:, :half], every[:, ys:, half:]], axis=1)
    start = jnp.zeros_like(right[0])
    exact = functools.partial(jnp.dot, precision=lax.Precision.HIGHEST)

    def up(state, inp):
        return exact(inp[0], state) + inp[1], state

    def down(state, inp):
        return exact(inp[0].T, state) + inp[1], state

    _, w = lax.scan(up, start, (maps, right))
    _, z = lax.scan(down, start, (maps, left), reverse=True)
    before, after = jnp.maximum(place - 1, 0), jnp.minimum(place + 1, count - 1)
    low = right[before] + lift_weight * (w[before] / xs + z[before])
    high = left[after] + lift_weight * (w[after] + z[after] / xs)
    low = jnp.where(place == 0, 0.0, low)
    high = jnp.where(place == count - 1, 0.0, high)
    return lift_weight * jnp.stack([w[place], z[place]]), jnp.stack([low, high]).astype(bf16)


def per_device(source, field, kerr, wave, leaf_ops, transfer_ops):
    xs, ys, cols = source.shape
    lx, ly, pts, _ = leaf_ops.shape
    points = xs // lx
    n_gx, n_gy = lax.axis_size("gx"), lax.axis_size("gy")
    paired = n_gx == 4
    shape = jax.ShapeDtypeStruct
    dots = 2 * lx * ly * pts * pts * cols

    edge_shape = (2, points, ys, cols)
    edges = shape(edge_shape, bf16)
    message = shape((ys + ys // 2, cols), bf16)
    far, near, edge, src, kerr_e = call(
        functools.partial(faces_body, paired, points, 1),
        (message, message, edges, edges, shape(edge_shape, f32)),
        [HBM] * 5,
        scratch=[
            pltpu.VMEM(edge_shape, bf16),
            pltpu.VMEM((2, ly, points, pts), bf16),
            pltpu.VMEM((xs, ys), f32),
            pltpu.VMEM((ys, ys), f32),
            pltpu.SemaphoreType.DMA((2, 2)),
            pltpu.SemaphoreType.DMA((4,)),
        ],
        cost=(dots // 8, 2 << 20),
    )(*map(in_hbm, (source, field, kerr, leaf_ops, transfer_ops)))

    if paired:
        sent = [(3, far), (2, far), (1, near)]
        got = [lax.ppermute(m, "gx", [(i, i ^ k) for i in range(n_gx)]) for k, m in sent]

    between = (xs - 2 * points, ys, cols)
    part, ends, mid, kerr_m, wave_b = call(
        functools.partial(leaves_body, points),
        (
            shape((xs * ys, cols), f32),
            shape((2 * xs, cols), f32),
            shape(between, bf16),
            shape(between, f32),
            shape((xs, ys, cols), f32),
        ),
        [VMEM] + [HBM] * 5,
        scratch=[
            pltpu.VMEM(between, bf16),
            pltpu.VMEM(between, bf16),
            pltpu.VMEM(leaf_ops.shape, bf16),
            pltpu.VMEM((2, xs, ys), f32),
            pltpu.SemaphoreType.DMA((4 + lx,)),
        ],
        cost=(dots, 6 << 20),
    )(edge, *map(in_hbm, (source, field, kerr, wave, leaf_ops)))

    column = shape((xs, cols), bf16)
    if paired:
        *got, part, ends = lax.optimization_barrier((*got, part, ends))
        waves, halo, pair, cross = call(
            finish_body,
            (shape((2, ys, cols), f32), shape((2, ys, cols), bf16), column, column),
            [VMEM] * 6,
        )(far, near, got[2], got[1], got[0], ends)
    else:
        waves, halo = gathered_sweeps(far, near, ys, xs, n_gx)
        pair, cross = call(ends_body, (column, column), [VMEM] * 2)(ends, waves)

    pair_to = [(i, i + 1 - 2 * (i % 2)) for i in range(n_gy)]
    cross_to = [(i, (i - 1 + 2 * (i % 2)) % n_gy) for i in range(n_gy)]
    pair = lax.ppermute(pair, "gy", pair_to)
    cross = lax.ppermute(cross, "gy", cross_to)

    strip, group, chunk, last = 8, 2, xs // 4, xs // 4
    big = shape((xs, ys, cols), bf16)
    updated, residual, strips, late = call(
        functools.partial(update_body, strip, group, chunk, last),
        (
            big,
            big,
            shape((2, xs, strip, cols), f32),
            shape((last, ys - 2 * strip, cols), bf16),
        ),
        [VMEM] * 8,
        out_specs=(ANY, ANY, VMEM, VMEM),
        scratch=[
            pltpu.VMEM((xs + 2, ys, cols), bf16),
            pltpu.VMEM((xs, ys - 2 * strip, cols), bf16),
            pltpu.SemaphoreType.DMA((2 * xs // chunk,)),
        ],
        cost=(20 * xs * ys * cols, 10 << 20),
    )(part, waves, halo, kerr_e, kerr_m, wave_b, src, mid)

    residual = call(
        functools.partial(seam_body, n_gy, strip, last),
        big,
        [VMEM] * 4 + [ANY],
        out_specs=ANY,
        scratch=[
            pltpu.VMEM((2, xs * strip, cols), f32),
            pltpu.VMEM((2, xs, strip, cols), bf16),
            pltpu.SemaphoreType.DMA((3,)),
        ],
        aliases={4: 0},
    )(strips, late, pair, cross, residual)
    return updated, residual


def solution(mesh):
    return jax.shard_map(
        per_device,
        mesh=mesh,
        in_specs=(
            P(("grp", "gx"), "gy", None),
            P(("grp", "gx"), "gy", None),
            P(("grp", "gx"), "gy"),
            P(("grp", "gx"), "gy"),
            P("gx", "gy", None, None),
            P("gx", "gy", None),
        ),
        out_specs=(P(("grp", "gx"), "gy", None), P(("grp", "gx"), "gy", None)),
        check_vma=False,
    )
```

```python
import functools

import jax
import jax.numpy as jnp
from jax import lax
from jax.experimental import pallas as pl
from jax.experimental.pallas import tpu as pltpu
from jax.sharding import PartitionSpec as P

lift_weight = 0.3
f32, bf16 = jnp.float32, jnp.bfloat16
VMEM = pl.BlockSpec(memory_space=pltpu.VMEM)
ANY = pl.BlockSpec(memory_space=pl.ANY)
HBM = pl.BlockSpec(memory_space=pltpu.HBM)


def call(body, outs, ins, out_specs=None, scratch=(), cost=(0, 0), aliases=None):
    def run(*args):
        return pl.pallas_call(
            body,
            out_shape=outs,
            in_specs=ins,
            out_specs=out_specs if out_specs is not None else jax.tree.map(lambda _: VMEM, outs),
            scratch_shapes=scratch,
            input_output_aliases=aliases or {},
            compiler_params=pltpu.CompilerParams(vmem_limit_bytes=24 << 20),
            cost_estimate=pl.CostEstimate(
                flops=cost[0], bytes_accessed=cost[1], transcendentals=0
            ),
        )(*args)

    return run


def in_hbm(x):
    return pltpu.with_memory_space_constraint(x, pltpu.HBM)


def matmul(a, b):
    return jnp.dot(a, b, preferred_element_type=f32)


def kerr_column(source, field, kerr):
    s, f = source.astype(f32), field.astype(f32)
    return (s - kerr * f * f * f).astype(bf16)


def seat(paired):
    if not paired:
        return True, True
    place = lax.axis_index("gx")
    return place < 2, (place == 1) | (place == 2)


def face(points, src, fld, ops, edge, kerr_e, e):
    ly, _, pts = ops.shape
    cols = src.shape[2]
    for q in range(points):
        edge[e, q] = kerr_column(src[q], fld[q], kerr_e[e, q])
    rows = []
    for b in range(ly):
        rhs = edge[e, :, b * points : (b + 1) * points, :].reshape(pts, cols)
        rows.append(matmul(ops[b], rhs))
    return jnp.concatenate(rows, axis=0).astype(bf16)


def toward_body(
    paired, points, source, field, kerr_all, leaf_ops, transfer,
    far, edge, src, kerr_e, fld, ops, kerr, fld_1, ops_1, own, sems,
):
    lx, ly, pts, _ = leaf_ops.shape
    xs, ys, cols = source.shape
    is_a, _ = seat(paired)
    e1 = jnp.where(is_a, 1, 0)
    e2 = 1 - e1
    copy = pltpu.make_async_copy

    def at_edge(e, f, o, sem):
        x0 = pl.multiple_of(e * (xs - points), points)
        r0 = pl.multiple_of(e * (pts - points), points)
        return [
            copy(source.at[pl.ds(x0, points)], src.at[e], sems.at[sem]),
            copy(field.at[pl.ds(x0, points)], f, sems.at[sem + 1]),
            copy(leaf_ops.at[e * (lx - 1), :, pl.ds(r0, points), :], o, sems.at[sem + 2]),
        ]

    coef = copy(kerr_all, kerr, sems.at[6])
    matrix = copy(transfer.at[0], own, sems.at[7])
    first = at_edge(e1, fld_1, ops_1, 0)
    second = at_edge(e2, fld, ops, 3)
    for c in [coef] + first + [matrix] + second:
        c.start()
    coef.wait()
    for e, x0 in enumerate((0, xs - points)):
        kt = kerr[x0 : x0 + points, :].T
        for q in range(points):
            kerr_e[e, q] = jnp.broadcast_to(kt[:, q : q + 1], (ys, cols))
    for c in first:
        c.wait()
    far[0:ys, :] = face(points, src.at[e1], fld_1, ops_1, edge, kerr_e, e1)
    matrix.wait()
    x_map = jnp.where(is_a, own[...], own[...].T).astype(bf16)
    far[ys:, :] = jnp.concatenate([x_map[: ys // 2], x_map[ys // 2 :]], axis=1)
    for c in second:
        c.wait()


def away_body(paired, points, far, src, fld, ops, kerr_e, edge_in, near, edge):
    ys = src.shape[2]
    is_a, inner = seat(paired)
    e2 = jnp.where(is_a, 0, 1)
    other = face(points, src.at[e2], fld, ops, edge, kerr_e, e2)
    near[0:ys, :] = jnp.where(inner, other, far[0:ys, :])
    near[ys:, :] = far[ys:, :]


def unpack(message):
    cols = message.shape[1]
    ys = 2 * message.shape[0] // 3
    packed = message[ys:]
    half = cols // 2
    return message[:ys], jnp.concatenate([packed[:, :half], packed[:, half:]], axis=0)


def leaves_body(
    points, edge, source, field, kerr, wave, leaf_ops, part, ends, mid, kerr_b, wave_b,
    fld, rhs, ops, coef, sems
):
    lx, ly, pts, _ = leaf_ops.shape
    xs, ys, cols = source.shape
    inner = pl.ds(points, xs - 2 * points)
    copy = pltpu.make_async_copy
    coefs = [copy(kerr, coef.at[0], sems.at[0]), copy(wave, coef.at[1], sems.at[1])]
    order = [0, lx - 1] + list(range(1, lx - 1))
    middle = [copy(source.at[inner], mid, sems.at[2]), copy(field.at[inner], fld, sems.at[3])]
    leaves = [copy(leaf_ops.at[a], ops.at[a], sems.at[4 + a]) for a in range(lx)]
    for c in coefs + [leaves[0], leaves[lx - 1]] + middle + leaves[1 : lx - 1]:
        c.start()

    def leaf_row(a, rows):
        leaves[a].wait()
        for b in range(ly):
            column = rows[:, b * points : (b + 1) * points, :].reshape(pts, cols)
            out = matmul(ops[a, b], column)
            for q in range(points):
                r = (a * points + q) * ys + b * points
                part[r : r + points, :] = out[q * points : (q + 1) * points, :]

    for c in coefs:
        c.wait()
    kt, wt = coef[0].T, coef[1].T

    def spread(out, i, columns, x):
        out[i] = jnp.broadcast_to(columns[:, x : x + 1], (ys, cols))

    for x in range(points, xs - points):
        spread(wave_b, x, wt, x)
    for a, rows in ((0, edge.at[0]), (lx - 1, edge.at[1])):
        leaf_row(a, rows)
        for x in range(a * points, (a + 1) * points):
            spread(wave_b, x, wt, x)
    for c in middle:
        c.wait()
    for a in order[2:]:
        for q in range(points):
            x, r = a * points + q, (a - 1) * points + q
            spread(kerr_b, r, kt, x)
            rhs[r] = kerr_column(mid[r], fld[r], kt[:, x : x + 1])
        leaf_row(a, rhs.at[pl.ds((a - 1) * points, points)])
    ends[0:xs, :] = part[pl.ds(0, xs, stride=ys), :]
    ends[xs:, :] = part[pl.ds(ys - 1, xs, stride=ys), :]


def profiles(xs):
    i = lax.broadcasted_iota(jnp.int32, (xs, 1), 0).astype(f32)
    return (xs - i) / xs, (i + 1.0) / xs


def edge_columns(ends, w, z, pair, cross):
    xs = pair.shape[0]
    ys = w.shape[0]
    lp, rp = profiles(xs)
    low = ends[0:xs, :] + (lp * w[0:1, :] + rp * z[0:1, :])
    high = ends[xs:, :] + (lp * w[ys - 1 : ys, :] + rp * z[ys - 1 : ys, :])
    even = lax.axis_index("gy") % 2 == 0
    pair[...] = jnp.where(even, high, low).astype(bf16)
    cross[...] = jnp.where(even, low, high).astype(bf16)


def finish_body(far, near, got_1, got_2, got_3, ends, waves, halo, pair, cross):
    xs = pair.shape[0]
    is_a, inner = seat(True)
    own_face, own_map = unpack(far[...])
    own_near, _ = unpack(near[...])
    mate_face, mate_map = unpack(got_1[...])
    face_2, map_2 = unpack(got_2[...])
    face_3, map_3 = unpack(got_3[...])
    other_map = jnp.where(inner, map_3, map_2)
    other_in = jnp.where(inner, face_3, face_2).astype(f32)
    other_out = jnp.where(inner, face_2, face_3)
    back_in = matmul(other_map, other_out) + other_in
    in_map = jnp.where(inner, own_map, mate_map)
    out_face = jnp.where(inner, mate_face, own_face)
    in_back = jnp.where(inner, own_near, mate_face).astype(f32)
    reach = matmul(in_map, out_face) + own_face.astype(f32)
    back_out = in_back + lax.dot_general(
        in_map, back_in.astype(bf16), (((0,), (0,)), ((), ())), preferred_element_type=f32
    )
    out_face, other_out = out_face.astype(f32), other_out.astype(f32)
    ahead = jnp.where(inner, out_face, 0.0)
    back = jnp.where(inner, back_in, back_out)
    w = lift_weight * jnp.where(is_a, ahead, back)
    z = lift_weight * jnp.where(is_a, back, ahead)
    waves[0] = w
    waves[1] = z
    edge_columns(ends, w, z, pair, cross)
    toward = jnp.where(
        inner,
        other_in + lift_weight * (reach + other_out * (1.0 / xs)),
        in_back + lift_weight * (out_face + back_in * (1.0 / xs)),
    )
    away = jnp.where(inner, out_face + lift_weight * back_out, 0.0)
    halo[0] = jnp.where(is_a, away, toward).astype(bf16)
    halo[1] = jnp.where(is_a, toward, away).astype(bf16)


def ends_body(ends, waves, pair, cross):
    edge_columns(ends, waves[0], waves[1], pair, cross)


def stencil(group, ys):
    shape = (group * ys, (group + 2) * ys)
    i = lax.broadcasted_iota(jnp.int32, shape, 0)
    j = lax.broadcasted_iota(jnp.int32, shape, 1)
    away = abs(i // ys + 1 - j // ys) + abs(i % ys - j % ys)
    return jnp.where(away == 0, -4.0, jnp.where(away == 1, 1.0, 0.0)).astype(bf16)


def update_body(
    strip, group, chunk, last, part, waves, halo, kerr_e, kerr_m, wave_b, src, mid, updated,
    residual, strips, late, u, res, sems,
):
    xs, ys, cols = updated.shape
    points = src.shape[1]

    def row(ends, middle, x):
        if x < points:
            return ends[0, x]
        return ends[1, x - xs + points] if x >= xs - points else middle[x - points]

    w, z = waves[0], waves[1]
    u[0] = halo[0]
    u[xs + 1] = halo[1]
    taps = stencil(group, ys)
    inside = pl.ds(strip, ys - 2 * strip)
    copies = []

    def send(src, dst):
        copies.append(pltpu.make_async_copy(src, dst, sems.at[len(copies)]))
        copies[-1].start()

    def lift(x, rise):
        u[x + 1] = (part[x * ys : (x + 1) * ys, :] + rise).astype(bf16)
        if (x + 1) % chunk == 0:
            at = pl.ds(x + 1 - chunk, chunk)
            send(u.at[pl.ds(x + 2 - chunk, chunk)], updated.at[at])

    def residue(x):
        near = matmul(taps, u[x : x + group + 2].reshape((group + 2) * ys, cols))
        for q in range(group):
            m = u[x + q + 1].astype(f32)
            s = row(src, mid, x + q).astype(f32)
            k = row(kerr_e, kerr_m, x + q)
            r = near[q * ys : (q + 1) * ys] + (m * (wave_b[x + q] + k * (m * m)) - s)
            strips[0, x + q] = r[:strip, :]
            strips[1, x + q] = r[ys - strip :, :]
            body = r[strip : ys - strip, :].astype(bf16)
            if x >= xs - last:
                late[x + q - (xs - last)] = body
            else:
                res[x + q] = body
        end = x + group
        if end % chunk == 0 and end <= xs - last:
            at = pl.ds(end - chunk, chunk)
            send(res.at[at], residual.at[at, inside])

    ahead = xs
    rise, slope = w + z * (1.0 / xs), (z - w) * (1.0 / xs)
    for x in range(xs + ahead):
        if x < xs:
            lift(x, rise)
            rise = rise + slope
        if x >= ahead and (x - ahead) % group == 0:
            residue(x - ahead)
    for c in copies:
        c.wait()


def seam_body(count, strip, last, strips, late, pair, cross, _, residual, work, out, sems):
    xs, ys, cols = residual.shape
    copies = [
        pltpu.make_async_copy(
            late,
            residual.at[pl.ds(xs - last, last), pl.ds(strip, ys - 2 * strip)],
            sems.at[2],
        )
    ]
    copies[0].start()
    g = lax.axis_index("gy")
    even = g % 2 == 0
    zero = jnp.zeros((), f32)
    p, c = pair[...].astype(f32), cross[...].astype(f32)
    low = jnp.where(g == 0, zero, jnp.where(even, c, p))
    high = jnp.where(g == count - 1, zero, jnp.where(even, p, c))
    for e, (row, add) in enumerate(((0, low), (strip - 1, high))):
        work[e] = strips[e].reshape(xs * strip, cols)
        at = pl.ds(row, xs, stride=strip)
        work[e, at, :] = work[e, at, :] + add
        out[e] = work[e].reshape(xs, strip, cols).astype(bf16)
        y0 = 0 if e == 0 else ys - strip
        copies.append(
            pltpu.make_async_copy(out.at[e], residual.at[:, pl.ds(y0, strip), :], sems.at[e])
        )
        copies[-1].start()
    for c in copies:
        c.wait()


def gathered_sweeps(far, near, ys, xs, count):
    place = lax.axis_index("gx")
    every, left = (lax.all_gather(m, "gx").astype(f32) for m in (far, near))
    right, left = every[:, :ys], left[:, :ys]
    half = every.shape[2] // 2
    maps = jnp.concatenate([every[:, ys:, :half], every[:, ys:, half:]], axis=1)
    start = jnp.zeros_like(right[0])
    exact = functools.partial(jnp.dot, precision=lax.Precision.HIGHEST)

    def up(state, inp):
        return exact(inp[0], state) + inp[1], state

    def down(state, inp):
        return exact(inp[0].T, state) + inp[1], state

    _, w = lax.scan(up, start, (maps, right))
    _, z = lax.scan(down, start, (maps, left), reverse=True)
    before, after = jnp.maximum(place - 1, 0), jnp.minimum(place + 1, count - 1)
    low = right[before] + lift_weight * (w[before] / xs + z[before])
    high = left[after] + lift_weight * (w[after] + z[after] / xs)
    low = jnp.where(place == 0, 0.0, low)
    high = jnp.where(place == count - 1, 0.0, high)
    return lift_weight * jnp.stack([w[place], z[place]]), jnp.stack([low, high]).astype(bf16)


def per_device(source, field, kerr, wave, leaf_ops, transfer_ops):
    xs, ys, cols = source.shape
    lx, ly, pts, _ = leaf_ops.shape
    points = xs // lx
    n_gx, n_gy = lax.axis_size("gx"), lax.axis_size("gy")
    paired = n_gx == 4
    shape = jax.ShapeDtypeStruct
    dots = 2 * lx * ly * pts * pts * cols

    edge_shape = (2, points, ys, cols)
    edges = shape(edge_shape, bf16)
    message = shape((ys + ys // 2, cols), bf16)
    rows = shape((ly, points, pts), bf16)
    part_edge = shape(edge_shape[1:], bf16)
    coefs = shape(edge_shape, f32)
    far, edge, src, kerr_e, fld, ops = call(
        functools.partial(toward_body, paired, points),
        (message, edges, edges, coefs, part_edge, rows),
        [HBM] * 5,
        scratch=[
            pltpu.VMEM((xs, ys), f32),
            pltpu.VMEM(part_edge.shape, bf16),
            pltpu.VMEM(rows.shape, bf16),
            pltpu.VMEM((ys, ys), f32),
            pltpu.SemaphoreType.DMA((8,)),
        ],
        cost=(dots // 16, 2 << 20),
    )(*map(in_hbm, (source, field, kerr, leaf_ops, transfer_ops)))
    near, edge = call(
        functools.partial(away_body, paired, points),
        (message, edges),
        [VMEM] * 6,
        aliases={5: 1},
        cost=(dots // 16, 1 << 20),
    )(far, src, fld, ops, kerr_e, edge)

    if paired:
        sent = [(3, far), (2, far), (1, near)]
        got = [lax.ppermute(m, "gx", [(i, i ^ k) for i in range(n_gx)]) for k, m in sent]

    between = (xs - 2 * points, ys, cols)
    part, ends, mid, kerr_m, wave_b = call(
        functools.partial(leaves_body, points),
        (
            shape((xs * ys, cols), f32),
            shape((2 * xs, cols), f32),
            shape(between, bf16),
            shape(between, f32),
            shape((xs, ys, cols), f32),
        ),
        [VMEM] + [HBM] * 5,
        scratch=[
            pltpu.VMEM(between, bf16),
            pltpu.VMEM(between, bf16),
            pltpu.VMEM(leaf_ops.shape, bf16),
            pltpu.VMEM((2, xs, ys), f32),
            pltpu.SemaphoreType.DMA((4 + lx,)),
        ],
        cost=(dots, 6 << 20),
    )(edge, *map(in_hbm, (source, field, kerr, wave, leaf_ops)))

    column = shape((xs, cols), bf16)
    if paired:
        *got, part, ends = lax.optimization_barrier((*got, part, ends))
        waves, halo, pair, cross = call(
            finish_body,
            (shape((2, ys, cols), f32), shape((2, ys, cols), bf16), column, column),
            [VMEM] * 6,
        )(far, near, got[2], got[1], got[0], ends)
    else:
        waves, halo = gathered_sweeps(far, near, ys, xs, n_gx)
        pair, cross = call(ends_body, (column, column), [VMEM] * 2)(ends, waves)

    pair_to = [(i, i + 1 - 2 * (i % 2)) for i in range(n_gy)]
    cross_to = [(i, (i - 1 + 2 * (i % 2)) % n_gy) for i in range(n_gy)]
    pair = lax.ppermute(pair, "gy", pair_to)
    cross = lax.ppermute(cross, "gy", cross_to)

    strip, group, chunk, last = 8, 2, xs // 4, xs // 4
    big = shape((xs, ys, cols), bf16)
    updated, residual, strips, late = call(
        functools.partial(update_body, strip, group, chunk, last),
        (
            big,
            big,
            shape((2, xs, strip, cols), f32),
            shape((last, ys - 2 * strip, cols), bf16),
        ),
        [VMEM] * 8,
        out_specs=(ANY, ANY, VMEM, VMEM),
        scratch=[
            pltpu.VMEM((xs + 2, ys, cols), bf16),
            pltpu.VMEM((xs, ys - 2 * strip, cols), bf16),
            pltpu.SemaphoreType.DMA((2 * xs // chunk,)),
        ],
        cost=(20 * xs * ys * cols, 10 << 20),
    )(part, waves, halo, kerr_e, kerr_m, wave_b, src, mid)

    residual = call(
        functools.partial(seam_body, n_gy, strip, last),
        big,
        [VMEM] * 4 + [ANY],
        out_specs=ANY,
        scratch=[
            pltpu.VMEM((2, xs * strip, cols), f32),
            pltpu.VMEM((2, xs, strip, cols), bf16),
            pltpu.SemaphoreType.DMA((3,)),
        ],
        aliases={4: 0},
    )(strips, late, pair, cross, residual)
    return updated, residual


def solution(mesh):
    return jax.shard_map(
        per_device,
        mesh=mesh,
        in_specs=(
            P(("grp", "gx"), "gy", None),
            P(("grp", "gx"), "gy", None),
            P(("grp", "gx"), "gy"),
            P(("grp", "gx"), "gy"),
            P("gx", "gy", None, None),
            P("gx", "gy", None),
        ),
        out_specs=(P(("grp", "gx"), "gy", None), P(("grp", "gx"), "gy", None)),
        check_vma=False,
    )
```

```python
import functools

import jax
import jax.numpy as jnp
from jax import lax
from jax.experimental import pallas as pl
from jax.experimental.pallas import tpu as pltpu
from jax.sharding import PartitionSpec as P

lift_weight = 0.3
f32, bf16 = jnp.float32, jnp.bfloat16
VMEM = pl.BlockSpec(memory_space=pltpu.VMEM)
ANY = pl.BlockSpec(memory_space=pl.ANY)
HBM = pl.BlockSpec(memory_space=pltpu.HBM)


def call(body, outs, ins, out_specs=None, scratch=(), cost=(0, 0), aliases=None):
    def run(*args):
        return pl.pallas_call(
            body,
            out_shape=outs,
            in_specs=ins,
            out_specs=out_specs if out_specs is not None else jax.tree.map(lambda _: VMEM, outs),
            scratch_shapes=scratch,
            input_output_aliases=aliases or {},
            compiler_params=pltpu.CompilerParams(vmem_limit_bytes=24 << 20),
            cost_estimate=pl.CostEstimate(
                flops=cost[0], bytes_accessed=cost[1], transcendentals=0
            ),
        )(*args)

    return run


def in_hbm(x):
    return pltpu.with_memory_space_constraint(x, pltpu.HBM)


def matmul(a, b):
    return jnp.dot(a, b, preferred_element_type=f32)


def kerr_column(source, field, kerr):
    s, f = source.astype(f32), field.astype(f32)
    return (s - kerr * f * f * f).astype(bf16)


def seat(paired):
    if not paired:
        return True, True
    place = lax.axis_index("gx")
    return place < 2, (place == 1) | (place == 2)


def face(points, src, fld, ops, coef, edge, kerr_e, e):
    ly, _, pts = ops.shape
    cols = src.shape[2]
    for q in range(points):
        kerr_e[e, q] = jnp.broadcast_to(coef[:, q : q + 1], src.shape[1:])
        edge[e, q] = kerr_column(src[q], fld[q], coef[:, q : q + 1])
    rows = []
    for b in range(ly):
        rhs = edge[e, :, b * points : (b + 1) * points, :].reshape(pts, cols)
        rows.append(matmul(ops[b], rhs))
    return jnp.concatenate(rows, axis=0).astype(bf16)


def toward_body(
    paired, points, source, field, kerr_all, leaf_ops, transfer,
    far, edge, src, kerr_e, fld, ops, kerr, fld_1, ops_1, own, sems,
):
    lx, ly, pts, _ = leaf_ops.shape
    xs, ys, cols = source.shape
    is_a, _ = seat(paired)
    e1 = jnp.where(is_a, 1, 0)
    e2 = 1 - e1
    copy = pltpu.make_async_copy

    def at_edge(e, f, o, sem):
        x0 = pl.multiple_of(e * (xs - points), points)
        r0 = pl.multiple_of(e * (pts - points), points)
        return [
            copy(source.at[pl.ds(x0, points)], src.at[e], sems.at[sem]),
            copy(field.at[pl.ds(x0, points)], f, sems.at[sem + 1]),
            copy(leaf_ops.at[e * (lx - 1), :, pl.ds(r0, points), :], o, sems.at[sem + 2]),
        ]

    coef = copy(kerr_all, kerr, sems.at[6])
    matrix = copy(transfer.at[0], own, sems.at[7])
    first = at_edge(e1, fld_1, ops_1, 0)
    second = at_edge(e2, fld, ops, 3)
    for c in [coef] + first + [matrix] + second:
        c.start()
    coef.wait()
    kt = kerr[pl.ds(pl.multiple_of(e1 * (xs - points), points), points), :].T
    for c in first:
        c.wait()
    far[0:ys, :] = face(points, src.at[e1], fld_1, ops_1, kt, edge, kerr_e, e1)
    matrix.wait()
    x_map = jnp.where(is_a, own[...], own[...].T).astype(bf16)
    far[ys:, :] = jnp.concatenate([x_map[: ys // 2], x_map[ys // 2 :]], axis=1)
    for c in second:
        c.wait()


def away_body(paired, points, far, src, fld, ops, kerr, edge_in, kerr_in, near, edge, kerr_e):
    xs, ys = kerr.shape
    is_a, inner = seat(paired)
    e2 = jnp.where(is_a, 0, 1)
    kt = kerr[pl.ds(pl.multiple_of(e2 * (xs - points), points), points), :].T
    other = face(points, src.at[e2], fld, ops, kt, edge, kerr_e, e2)
    near[0:ys, :] = jnp.where(inner, other, far[0:ys, :])
    near[ys:, :] = far[ys:, :]


def unpack(message):
    cols = message.shape[1]
    ys = 2 * message.shape[0] // 3
    packed = message[ys:]
    half = cols // 2
    return message[:ys], jnp.concatenate([packed[:, :half], packed[:, half:]], axis=0)


def leaves_body(
    points, edge, source, field, kerr, wave, leaf_ops, part, ends, mid, kerr_b, wave_b,
    fld, rhs, ops, coef, sems
):
    lx, ly, pts, _ = leaf_ops.shape
    xs, ys, cols = source.shape
    inner = pl.ds(points, xs - 2 * points)
    copy = pltpu.make_async_copy
    coefs = [copy(kerr, coef.at[0], sems.at[0]), copy(wave, coef.at[1], sems.at[1])]
    order = [0, lx - 1] + list(range(1, lx - 1))
    middle = [copy(source.at[inner], mid, sems.at[2]), copy(field.at[inner], fld, sems.at[3])]
    leaves = [copy(leaf_ops.at[a], ops.at[a], sems.at[4 + a]) for a in range(lx)]
    for c in coefs + [leaves[0], leaves[lx - 1]] + middle + leaves[1 : lx - 1]:
        c.start()

    def leaf_row(a, rows):
        leaves[a].wait()
        for b in range(ly):
            column = rows[:, b * points : (b + 1) * points, :].reshape(pts, cols)
            out = matmul(ops[a, b], column)
            for q in range(points):
                r = (a * points + q) * ys + b * points
                part[r : r + points, :] = out[q * points : (q + 1) * points, :]

    for c in coefs:
        c.wait()
    kt, wt = coef[0].T, coef[1].T

    def spread(out, i, columns, x):
        out[i] = jnp.broadcast_to(columns[:, x : x + 1], (ys, cols))

    for x in range(points, xs - points):
        spread(wave_b, x, wt, x)
    for a, rows in ((0, edge.at[0]), (lx - 1, edge.at[1])):
        leaf_row(a, rows)
        for x in range(a * points, (a + 1) * points):
            spread(wave_b, x, wt, x)
    for c in middle:
        c.wait()
    for a in order[2:]:
        for q in range(points):
            x, r = a * points + q, (a - 1) * points + q
            spread(kerr_b, r, kt, x)
            rhs[r] = kerr_column(mid[r], fld[r], kt[:, x : x + 1])
        leaf_row(a, rhs.at[pl.ds((a - 1) * points, points)])
    ends[0:xs, :] = part[pl.ds(0, xs, stride=ys), :]
    ends[xs:, :] = part[pl.ds(ys - 1, xs, stride=ys), :]


def profiles(xs):
    i = lax.broadcasted_iota(jnp.int32, (xs, 1), 0).astype(f32)
    return (xs - i) / xs, (i + 1.0) / xs


def edge_columns(ends, w, z, pair, cross):
    xs = pair.shape[0]
    ys = w.shape[0]
    lp, rp = profiles(xs)
    low = ends[0:xs, :] + (lp * w[0:1, :] + rp * z[0:1, :])
    high = ends[xs:, :] + (lp * w[ys - 1 : ys, :] + rp * z[ys - 1 : ys, :])
    even = lax.axis_index("gy") % 2 == 0
    pair[...] = jnp.where(even, high, low).astype(bf16)
    cross[...] = jnp.where(even, low, high).astype(bf16)


def finish_body(far, near, got_1, got_2, got_3, ends, waves, halo, pair, cross):
    xs = pair.shape[0]
    is_a, inner = seat(True)
    ys = got_1.shape[0] * 2 // 3
    mine, mate, second, third = far[...], got_1[...], got_2[...], got_3[...]
    other_in, other_map = unpack(jnp.where(inner, third, second))
    other_out = jnp.where(inner, second[:ys], third[:ys])
    other_in = other_in.astype(f32)
    back_in = matmul(other_map, other_out) + other_in
    _, in_map = unpack(jnp.where(inner, mine, mate))
    out_face = jnp.where(inner, mate[:ys], mine[:ys])
    in_back = jnp.where(inner, near[0:ys, :], mate[:ys]).astype(f32)
    reach = matmul(in_map, out_face) + mine[:ys].astype(f32)
    back_out = in_back + matmul(in_map.astype(f32).T.astype(bf16), back_in.astype(bf16))
    out_face, other_out = out_face.astype(f32), other_out.astype(f32)
    ahead = jnp.where(inner, out_face, 0.0)
    back = jnp.where(inner, back_in, back_out)
    w = lift_weight * jnp.where(is_a, ahead, back)
    z = lift_weight * jnp.where(is_a, back, ahead)
    waves[0] = w
    waves[1] = z
    edge_columns(ends, w, z, pair, cross)
    toward = jnp.where(
        inner,
        other_in + lift_weight * (reach + other_out * (1.0 / xs)),
        in_back + lift_weight * (out_face + back_in * (1.0 / xs)),
    )
    away = jnp.where(inner, out_face + lift_weight * back_out, 0.0)
    halo[0] = jnp.where(is_a, away, toward).astype(bf16)
    halo[1] = jnp.where(is_a, toward, away).astype(bf16)


def ends_body(ends, waves, pair, cross):
    edge_columns(ends, waves[0], waves[1], pair, cross)


def stencil(group, ys):
    shape = (group * ys, (group + 2) * ys)
    i = lax.broadcasted_iota(jnp.int32, shape, 0)
    j = lax.broadcasted_iota(jnp.int32, shape, 1)
    away = abs(i // ys + 1 - j // ys) + abs(i % ys - j % ys)
    return jnp.where(away == 0, -4.0, jnp.where(away == 1, 1.0, 0.0)).astype(bf16)


def update_body(
    strip, group, chunk, last, part, waves, halo, kerr_e, kerr_m, wave_b, src, mid, updated,
    residual, strips, late, u, res, sems,
):
    xs, ys, cols = updated.shape
    points = src.shape[1]

    def row(ends, middle, x):
        if x < points:
            return ends[0, x]
        return ends[1, x - xs + points] if x >= xs - points else middle[x - points]

    w, z = waves[0], waves[1]
    u[0] = halo[0]
    u[xs + 1] = halo[1]
    taps = stencil(group, ys)
    inside = pl.ds(strip, ys - 2 * strip)
    copies = []

    def send(src, dst):
        copies.append(pltpu.make_async_copy(src, dst, sems.at[len(copies)]))
        copies[-1].start()

    def lift(x, rise):
        u[x + 1] = (part[x * ys : (x + 1) * ys, :] + rise).astype(bf16)
        if (x + 1) % chunk == 0:
            at = pl.ds(x + 1 - chunk, chunk)
            send(u.at[pl.ds(x + 2 - chunk, chunk)], updated.at[at])

    def residue(x):
        near = matmul(taps, u[x : x + group + 2].reshape((group + 2) * ys, cols))
        for q in range(group):
            m = u[x + q + 1].astype(f32)
            s = row(src, mid, x + q).astype(f32)
            k = row(kerr_e, kerr_m, x + q)
            r = near[q * ys : (q + 1) * ys] + (m * (wave_b[x + q] + k * (m * m)) - s)
            strips[0, x + q] = r[:strip, :]
            strips[1, x + q] = r[ys - strip :, :]
            body = r[strip : ys - strip, :].astype(bf16)
            if x >= xs - last:
                late[x + q - (xs - last)] = body
            else:
                res[x + q] = body
        end = x + group
        if end % chunk == 0 and end <= xs - last:
            at = pl.ds(end - chunk, chunk)
            send(res.at[at], residual.at[at, inside])

    ahead = xs
    rise, slope = w + z * (1.0 / xs), (z - w) * (1.0 / xs)
    for x in range(xs + ahead):
        if x < xs:
            lift(x, rise)
            rise = rise + slope
        if x >= ahead and (x - ahead) % group == 0:
            residue(x - ahead)
    for c in copies:
        c.wait()


def seam_body(count, strip, last, strips, late, pair, cross, _, residual, work, out, sems):
    xs, ys, cols = residual.shape
    copies = [
        pltpu.make_async_copy(
            late,
            residual.at[pl.ds(xs - last, last), pl.ds(strip, ys - 2 * strip)],
            sems.at[2],
        )
    ]
    copies[0].start()
    g = lax.axis_index("gy")
    even = g % 2 == 0
    zero = jnp.zeros((), f32)
    p, c = pair[...].astype(f32), cross[...].astype(f32)
    low = jnp.where(g == 0, zero, jnp.where(even, c, p))
    high = jnp.where(g == count - 1, zero, jnp.where(even, p, c))
    for e, (row, add) in enumerate(((0, low), (strip - 1, high))):
        work[e] = strips[e].reshape(xs * strip, cols)
        at = pl.ds(row, xs, stride=strip)
        work[e, at, :] = work[e, at, :] + add
        out[e] = work[e].reshape(xs, strip, cols).astype(bf16)
        y0 = 0 if e == 0 else ys - strip
        copies.append(
            pltpu.make_async_copy(out.at[e], residual.at[:, pl.ds(y0, strip), :], sems.at[e])
        )
        copies[-1].start()
    for c in copies:
        c.wait()


def gathered_sweeps(far, near, ys, xs, count):
    place = lax.axis_index("gx")
    every, left = (lax.all_gather(m, "gx").astype(f32) for m in (far, near))
    right, left = every[:, :ys], left[:, :ys]
    half = every.shape[2] // 2
    maps = jnp.concatenate([every[:, ys:, :half], every[:, ys:, half:]], axis=1)
    start = jnp.zeros_like(right[0])
    exact = functools.partial(jnp.dot, precision=lax.Precision.HIGHEST)

    def up(state, inp):
        return exact(inp[0], state) + inp[1], state

    def down(state, inp):
        return exact(inp[0].T, state) + inp[1], state

    _, w = lax.scan(up, start, (maps, right))
    _, z = lax.scan(down, start, (maps, left), reverse=True)
    before, after = jnp.maximum(place - 1, 0), jnp.minimum(place + 1, count - 1)
    low = right[before] + lift_weight * (w[before] / xs + z[before])
    high = left[after] + lift_weight * (w[after] + z[after] / xs)
    low = jnp.where(place == 0, 0.0, low)
    high = jnp.where(place == count - 1, 0.0, high)
    return lift_weight * jnp.stack([w[place], z[place]]), jnp.stack([low, high]).astype(bf16)


def per_device(source, field, kerr, wave, leaf_ops, transfer_ops):
    xs, ys, cols = source.shape
    lx, ly, pts, _ = leaf_ops.shape
    points = xs // lx
    n_gx, n_gy = lax.axis_size("gx"), lax.axis_size("gy")
    paired = n_gx == 4
    shape = jax.ShapeDtypeStruct
    dots = 2 * lx * ly * pts * pts * cols

    edge_shape = (2, points, ys, cols)
    edges = shape(edge_shape, bf16)
    message = shape((ys + ys // 2, cols), bf16)
    rows = shape((ly, points, pts), bf16)
    part_edge = shape(edge_shape[1:], bf16)
    coefs = shape(edge_shape, f32)
    far, edge, src, kerr_e, fld, ops, kerr_v = call(
        functools.partial(toward_body, paired, points),
        (message, edges, edges, coefs, part_edge, rows, shape((xs, ys), f32)),
        [HBM] * 5,
        scratch=[
            pltpu.VMEM(part_edge.shape, bf16),
            pltpu.VMEM(rows.shape, bf16),
            pltpu.VMEM((ys, ys), f32),
            pltpu.SemaphoreType.DMA((8,)),
        ],
        cost=(dots // 16, 2 << 20),
    )(*map(in_hbm, (source, field, kerr, leaf_ops, transfer_ops)))
    near, edge, kerr_e = call(
        functools.partial(away_body, paired, points),
        (message, edges, coefs),
        [VMEM] * 7,
        aliases={5: 1, 6: 2},
        cost=(dots // 16, 1 << 20),
    )(far, src, fld, ops, kerr_v, edge, kerr_e)

    if paired:
        sent = [(2, far), (3, far), (1, near)]
        got = [lax.ppermute(m, "gx", [(i, i ^ k) for i in range(n_gx)]) for k, m in sent]

    between = (xs - 2 * points, ys, cols)
    part, ends, mid, kerr_m, wave_b = call(
        functools.partial(leaves_body, points),
        (
            shape((xs * ys, cols), f32),
            shape((2 * xs, cols), f32),
            shape(between, bf16),
            shape(between, f32),
            shape((xs, ys, cols), f32),
        ),
        [VMEM] + [HBM] * 5,
        scratch=[
            pltpu.VMEM(between, bf16),
            pltpu.VMEM(between, bf16),
            pltpu.VMEM(leaf_ops.shape, bf16),
            pltpu.VMEM((2, xs, ys), f32),
            pltpu.SemaphoreType.DMA((4 + lx,)),
        ],
        cost=(dots, 6 << 20),
    )(edge, *map(in_hbm, (source, field, kerr, wave, leaf_ops)))

    column = shape((xs, cols), bf16)
    if paired:
        *got, part, ends = lax.optimization_barrier((*got, part, ends))
        waves, halo, pair, cross = call(
            finish_body,
            (shape((2, ys, cols), f32), shape((2, ys, cols), bf16), column, column),
            [VMEM] * 6,
        )(far, near, got[2], got[0], got[1], ends)
    else:
        waves, halo = gathered_sweeps(far, near, ys, xs, n_gx)
        pair, cross = call(ends_body, (column, column), [VMEM] * 2)(ends, waves)

    pair_to = [(i, i + 1 - 2 * (i % 2)) for i in range(n_gy)]
    cross_to = [(i, (i - 1 + 2 * (i % 2)) % n_gy) for i in range(n_gy)]
    pair = lax.ppermute(pair, "gy", pair_to)
    cross = lax.ppermute(cross, "gy", cross_to)

    strip, group, chunk, last = 8, 2, xs // 4, xs // 4
    big = shape((xs, ys, cols), bf16)
    updated, residual, strips, late = call(
        functools.partial(update_body, strip, group, chunk, last),
        (
            big,
            big,
            shape((2, xs, strip, cols), f32),
            shape((last, ys - 2 * strip, cols), bf16),
        ),
        [VMEM] * 8,
        out_specs=(ANY, ANY, VMEM, VMEM),
        scratch=[
            pltpu.VMEM((xs + 2, ys, cols), bf16),
            pltpu.VMEM((xs, ys - 2 * strip, cols), bf16),
            pltpu.SemaphoreType.DMA((2 * xs // chunk,)),
        ],
        cost=(20 * xs * ys * cols, 10 << 20),
    )(part, waves, halo, kerr_e, kerr_m, wave_b, src, mid)

    residual = call(
        functools.partial(seam_body, n_gy, strip, last),
        big,
        [VMEM] * 4 + [ANY],
        out_specs=ANY,
        scratch=[
            pltpu.VMEM((2, xs * strip, cols), f32),
            pltpu.VMEM((2, xs, strip, cols), bf16),
            pltpu.SemaphoreType.DMA((3,)),
        ],
        aliases={4: 0},
    )(strips, late, pair, cross, residual)
    return updated, residual


def solution(mesh):
    return jax.shard_map(
        per_device,
        mesh=mesh,
        in_specs=(
            P(("grp", "gx"), "gy", None),
            P(("grp", "gx"), "gy", None),
            P(("grp", "gx"), "gy"),
            P(("grp", "gx"), "gy"),
            P("gx", "gy", None, None),
            P("gx", "gy", None),
        ),
        out_specs=(P(("grp", "gx"), "gy", None), P(("grp", "gx"), "gy", None)),
        check_vma=False,
    )
```
